128 devices in a mesh: var: 16 (over x, z), samp: 8 (over y, core).
Axes of the slice: x: 4, y: 4, z: 4, core: 2. Of those that a mesh axis runs over, the one named last changes fastest.
Arguments:
- data: bfloat16 [2048, 32768], P('samp', 'var'), may hold values from -6 to 6
- omega: float32 [256, 8, 128, 128], P('var'), may hold values from -1.2 to 3, as said below
- pattern: int32 [256, 8], P('var'), may hold values from 0 to 255, as said below
- counts: int32 [256], P('var'), may hold values from 2 to 8, as said below
Outputs:
- omega_next: float32 [256, 8, 128, 128], P('var', None, 'samp')
The draws below stay inside these ranges and needn't reach their ends.
Inputs may be any that keep to these rules, and one draw needn't show every extreme that they name: pattern[r, 0] = r; the live slots of a row name distinct blocks, each owned by the same index of var as r, by a neighbouring one, or a hub block (a block whose row has all 8 slots live); dead slots also name such blocks. `counts`: exactly 2 block rows of each index of var, the hub blocks, have all 8 slots live; the others from 2 to 4. `omega`: diagonal entries of slot 0 lie in 1 to 3; tiles of dead slots hold values that are not part of Omega.
All inputs are finite; a program needn't handle non-finite values.
Results may differ from the reference program's by a relative error of at most 0.00045.
Values may be sent and summed in bfloat16 or wider, within the bound.
No kernel may reach another device: no remote copies, remote signals or barrier semaphores. Data moves between devices by JAX's collectives and lax.ppermute only.
A program may use at most 192 MiB of HBM per device.

```python
import jax
import jax.numpy as jnp
from jax import lax

BS = 128
KMAX = 8
HUB_DEV = 2
ITERS = 2
BR_DEV = 16
NB = 256
VOXELS = 32768
SAMPLES = 2048


def layout(key):
    folded = jax.random.fold_in(key, 11)
    key_hub, key_count, key_score = jax.random.split(folded, 3)
    var_count = NB // BR_DEV
    orders = jax.vmap(lambda single: jax.random.permutation(single, BR_DEV))(jax.random.split(key_hub, var_count))
    hub_list = (jnp.arange(var_count, dtype=jnp.int32)[:, None] * BR_DEV + orders[:, :HUB_DEV].astype(jnp.int32)).reshape(-1)
    blocks = jnp.arange(NB, dtype=jnp.int32)
    is_hub = jnp.any(blocks[:, None] == hub_list[None, :], axis=1)
    live_counts = jax.random.randint(key_count, (NB,), KMAX // 4, KMAX // 2 + 1, dtype=jnp.int32)
    live_counts = jnp.where(is_hub, KMAX, live_counts).astype(jnp.int32)
    owners = blocks // BR_DEV
    nearby = jnp.abs(owners[:, None] - owners[None, :]) <= 1
    eligible = (nearby | is_hub[None, :]) & (blocks[:, None] != blocks[None, :])
    random_score = jax.random.randint(key_score, (NB, NB), 0, 2 ** 20, dtype=jnp.int32)
    ranking = jnp.where(eligible, random_score * NB + blocks[None, :], -1 - blocks[None, :])
    chosen = lax.top_k(ranking, KMAX - 1)[1].astype(jnp.int32)
    pattern_table = jnp.concatenate([blocks[:, None], chosen], axis=1)
    return (pattern_table, live_counts)


def draw_pattern(key, part):
    return layout(key)[0]


def draw_counts(key, part):
    return layout(key)[1]


def draw_omega(key, part):
    key_spread, key_diagonal = jax.random.split(jax.random.fold_in(key, 5))
    shape = (NB, KMAX, BS, BS)
    spread = 0.3 * jax.random.truncated_normal(key_spread, -4.0, 4.0, shape, jnp.float32)
    diagonal = jax.random.uniform(key_diagonal, (NB, BS), jnp.float32, 1.0, 3.0)
    identity = jnp.arange(BS)[:, None] == jnp.arange(BS)[None, :]
    leading = (jnp.arange(KMAX) == 0)[None, :, None, None] & identity[None, None]
    return jnp.where(leading, diagonal[:, None, :, None], spread).astype(jnp.float32)


def levels(own_key, dims, cuts, smallest, top_value):
    def one(position, shards_of):
        heights = jax.random.uniform(jax.random.fold_in(jax.random.fold_in(own_key, 6), position), (shards_of,), jnp.float32, smallest / len(cuts), top_value / len(cuts))
        return jnp.repeat(jnp.exp(heights), dims[position] // shards_of).reshape((-1,) + (1,) * (len(dims) - position - 1))

    factor_of = one(*cuts[0])
    for cut in cuts[1:]:
        factor_of = factor_of * one(*cut)
    return factor_of


def normal_values(own_key, shape, width, limit, cuts=(), kind=jnp.bfloat16):
    loudness = levels(own_key, shape, cuts, -0.22, 0.18) if cuts else 1.0
    drawn = jax.random.normal(own_key, shape, jnp.float32) * width * loudness
    return jnp.minimum(jnp.maximum(drawn, -limit), limit).astype(kind)


def setup_inputs(seed: int = 0) -> dict:
    key_list = jax.random.split(jax.random.key(seed), 5)
    data = normal_values(key_list[0], (SAMPLES, VOXELS), 1.0, 6.0, ((0, 8), (1, 16)))
    omega = draw_omega(jax.random.fold_in(key_list[4], 71), 0)
    pattern = draw_pattern(jax.random.fold_in(key_list[4], 71), 0)
    counts = draw_counts(jax.random.fold_in(key_list[4], 71), 0)
    return {"data": data, "omega": omega, "pattern": pattern, "counts": counts}


STEP_SIZE = 0.25
PENALTY = 1.0
HIGHEST = lax.Precision.HIGHEST

def prox_update(current, gradient, slot_live, row_start):
    block_count, slot_count, height, block_size = current.shape
    stepped = current - STEP_SIZE * gradient
    row_index = row_start + lax.broadcasted_iota(jnp.int32, (height, block_size), 0)
    col_index = lax.broadcasted_iota(jnp.int32, (height, block_size), 1)
    leading = lax.broadcasted_iota(jnp.int32, (slot_count, 1, 1), 0) == 0
    diagonal = leading & (row_index == col_index)[None]
    shrunk = jnp.sign(stepped) * jnp.maximum(jnp.abs(stepped) - STEP_SIZE * PENALTY, 0.0)
    barrier = 0.5 * (stepped + jnp.sqrt(stepped * stepped + 4.0 * STEP_SIZE))
    return jnp.where(diagonal[None], barrier, shrunk) * slot_live[:, :, None, None]

def reference(data, omega, pattern, counts):
    block_count, slot_count, block_size, _ = omega.shape
    all_samples = data.shape[0]
    xblocks = data.astype(jnp.float32).reshape(all_samples, block_count, block_size).transpose(1, 0, 2)
    slot_live = (lax.broadcasted_iota(jnp.int32, (block_count, slot_count), 1) < counts[:, None]).astype(jnp.float32)
    current = omega
    for iteration in range(ITERS):
        masked = current * slot_live[:, :, None, None]

        def image_row(args):
            tiles, columns = args
            return jnp.einsum('kij,knj->in', tiles, xblocks[columns], precision=HIGHEST)
        images = lax.map(image_row, (masked, pattern))

        def gradient_row(args):
            own_image, own_x, columns = args
            first_term = jnp.einsum('in,knj->kij', own_image, xblocks[columns], precision=HIGHEST)
            second_term = jnp.einsum('ni,kjn->kij', own_x, images[columns], precision=HIGHEST)
            return (first_term + second_term) * (0.5 / all_samples)
        gradient = lax.map(gradient_row, (images, xblocks, pattern))
        current = prox_update(current, gradient, slot_live, 0)
    return current
```

```python
import jax
import jax.numpy as jnp
from jax import lax
from jax.experimental import pallas as pl
from jax.experimental.pallas import tpu as pltpu
from jax.sharding import PartitionSpec as P

HUB_DEV = 2
ITERS = 2
STEP_SIZE = 0.25
PENALTY = 1.0
HALF = 4
GROUP = 4
SIDE = 4
CORES = 2
BF = jnp.bfloat16
F32 = jnp.float32
ANY = pl.BlockSpec(memory_space=pl.ANY)
SMEM = pl.BlockSpec(memory_space=pltpu.SMEM)
VMEM = pl.BlockSpec(memory_space=pltpu.VMEM)


def var_shift(dx, dz):
    return [
        (x * SIDE + z, ((x + dx) % SIDE) * SIDE + (z + dz) % SIDE)
        for x in range(SIDE)
        for z in range(SIDE)
    ]


def samp_shift(dy, dc):
    return [
        (y * CORES + c, ((y + dy) % SIDE) * CORES + (c + dc) % CORES)
        for y in range(SIDE)
        for c in range(CORES)
    ]


def row_order(counts, order, slots):
    def step(r, carry):
        hubs, others = carry
        hub = jnp.where(counts[r] == slots, 1, 0)
        order[jnp.where(hub == 1, hubs, HUB_DEV + others)] = r
        return hubs + hub, others + 1 - hub

    lax.fori_loop(0, order.shape[0], step, (jnp.int32(0), jnp.int32(0)))


def slot_base(p, slots):
    return p * slots if p < HUB_DEV else HUB_DEV * slots + (p - HUB_DEV) * HALF


def aligned(index, size):
    return pl.ds(pl.multiple_of(index * size, size), size)


def pack_kernel(slots, counts, data, other_out, hub_out, order):
    rows = order.shape[0]
    bs = other_out.shape[1]
    row_order(counts, order, slots)
    first = lax.axis_index("var") * rows
    shape = (bs, bs)
    eye = lax.broadcasted_iota(jnp.int32, shape, 0) == lax.broadcasted_iota(jnp.int32, shape, 1)
    eye = eye.astype(F32).astype(BF)
    for p in range(rows):
        block = data[:, aligned(order[p], bs)]
        turned = lax.dot_general(
            eye, block, (((1,), (1,)), ((), ())), preferred_element_type=F32
        ).astype(BF)
        if p < HUB_DEV:
            hub_out[p * bs : (p + 1) * bs, :] = turned
        else:
            other_out[p - HUB_DEV] = turned
    tail = hub_out.shape[0] - HUB_DEV * bs
    lead = lax.broadcasted_iota(jnp.int32, (tail, hub_out.shape[1]), 0) == 0
    ids = jnp.where(lead, first + order[0], first + order[1])
    hub_out[HUB_DEV * bs :, :] = ids.astype(F32).astype(BF)


def pack(data, counts, slots, bs):
    rows = counts.shape[0]
    local = data.shape[0]
    return pl.pallas_call(
        lambda *refs: pack_kernel(slots, *refs),
        out_shape=(
            jax.ShapeDtypeStruct((rows - HUB_DEV, bs, local), BF),
            jax.ShapeDtypeStruct((HUB_DEV * bs + 16, local), BF),
        ),
        in_specs=[SMEM, VMEM],
        out_specs=(VMEM, VMEM),
        scratch_shapes=[pltpu.SMEM((rows,), jnp.int32)],
        name="pack",
    )(counts, data)


def table_copies(near, hubs, table, sem):
    copies = []
    at = 0
    for ref in near:
        size = ref.shape[0] * ref.shape[1]
        copies.append((ref.reshape(size, ref.shape[2]), table.at[pl.ds(at, size), :]))
        at += size
    for ref in hubs:
        if len(ref.shape) == 3:
            size = HUB_DEV * (ref.shape[1] // HUB_DEV // 128) * 128
            for z in range(ref.shape[0]):
                copies.append((ref.at[z, pl.ds(0, size), :], table.at[pl.ds(at, size), :]))
                at += size
        else:
            raise ValueError
    return [pltpu.make_async_copy(a, b, sem) for a, b in copies]


def fill_lookup(counts, pattern, ids, order, inverse, lookup):
    rows, slots = pattern.shape
    plain = rows - HUB_DEV
    base = lax.axis_index("var") * rows

    def clear(i, _):
        inverse[base + i] = -1
        return 0

    lax.fori_loop(0, 3 * rows, clear, 0)

    def mark(q, _):
        inverse[ids[q] + rows] = 3 * plain + q
        return 0

    lax.fori_loop(0, ids.shape[0], mark, 0)
    for side in range(3):

        def place(i, found):
            at = base + side * rows + i
            seen = inverse[at]
            inverse[at] = jnp.where(seen < 0, side * plain + found, seen)
            return found + jnp.where(seen < 0, 1, 0)

        lax.fori_loop(0, rows, place, jnp.int32(0))
    total = 3 * plain + ids.shape[0]
    for p in range(rows):
        for k in range(slots if p < HUB_DEV else HALF):
            c = inverse[pattern[order[p], k] + rows]
            lookup[slot_base(p, slots) + k] = jnp.clip(c, 0, total - 1)


def image_rows(counts, order, lookup, tile_of, table, other_out, hub_out, slots):
    bs = other_out.shape[1]
    rows = order.shape[0]

    def group(start, live):
        high, low, blocks = [], [], []
        for k in range(GROUP):
            tile = jnp.where(k < live, tile_of(start + k), 0.0)
            top = tile.astype(BF)
            high.append(top)
            low.append((tile - top.astype(F32)).astype(BF))
            blocks.append(table[aligned(lookup[start + k], bs), :])
        left = jnp.concatenate(
            [jnp.concatenate(high, axis=1), jnp.concatenate(low, axis=1)], axis=0
        )
        both = jnp.dot(left, jnp.concatenate(blocks, axis=0), preferred_element_type=F32)
        return both[:bs] + both[bs:]

    for p in range(HUB_DEV):
        total = group(p * slots, GROUP) + group(p * slots + GROUP, GROUP)
        hub_out[p * bs : (p + 1) * bs, :] = total.astype(BF)

    def plain(p, _):
        image = group(HUB_DEV * slots + p * HALF, counts[order[HUB_DEV + p]])
        other_out[p] = image.astype(BF)
        return 0

    lax.fori_loop(0, rows - HUB_DEV, plain, 0)


def first_image_kernel(*refs):
    counts, pattern, ids, omega = refs[:4]
    near, hubs = refs[4:7], refs[7:11]
    other_out, hub_out, lookup, rows_out = refs[11:15]
    order, inverse, table, tiles, table_sem, tile_sem = refs[15:]
    rows, slots = pattern.shape
    share = rows_out.shape[1]
    row_order(counts, order, slots)
    moves = table_copies(near, hubs, table, table_sem)
    for move in moves:
        move.start()
    tile_moves = []
    for p in range(rows):
        n = slots if p < HUB_DEV else HALF
        tile_moves.append(
            pltpu.make_async_copy(
                omega.at[order[p], pl.ds(0, n)],
                tiles.at[pl.ds(slot_base(p, slots), n)],
                tile_sem,
            )
        )
        tile_moves[-1].start()
    fill_lookup(counts, pattern, ids, order, inverse, lookup)
    for move in tile_moves + moves:
        move.wait()
    image_rows(counts, order, lookup, lambda s: tiles[s], table, other_out, hub_out, slots)
    part = lax.axis_index("samp")

    def keep(s, _):
        rows_out[s] = tiles[s, aligned(part, share), :]
        return 0

    lax.fori_loop(0, rows_out.shape[0], keep, 0)


def later_image_kernel(*refs):
    counts, lookup, mine, partner = refs[:4]
    near, hubs = refs[4:7], refs[7:11]
    other_out, hub_out = refs[11:13]
    order, table, tiles, table_sem, tile_sem = refs[13:]
    rows = order.shape[0]
    slots = (lookup.shape[0] - (rows - HUB_DEV) * HALF) // HUB_DEV
    share = mine.shape[2]
    row_order(counts, order, slots)
    moves = table_copies(near, hubs, table, table_sem)
    part = lax.axis_index("samp")
    for j in range(SIDE):
        for ref, core in ((mine, part % CORES), (partner, (part + 1) % CORES)):
            at = ((part // CORES + j) % SIDE) * CORES + core
            moves.append(
                pltpu.make_async_copy(ref.at[j], tiles.at[:, aligned(at, share), :], tile_sem)
            )
    for move in moves:
        move.start()
    for move in moves:
        move.wait()
    image_rows(counts, order, lookup, lambda s: tiles[s], table, other_out, hub_out, slots)


def image_shapes(near):
    plain, bs, local = near[0].shape
    return (
        jax.ShapeDtypeStruct((plain, bs, local), BF),
        jax.ShapeDtypeStruct((HUB_DEV * bs, local), BF),
    )


def table_rows(near, hubs):
    plain, bs, _ = near[0].shape
    return (3 * plain + len(hubs) * hubs[0].shape[0] * HUB_DEV) * bs


def first_image(counts, pattern, ids, omega, near, hubs, part_count):
    rows, slots, bs, _ = omega.shape
    total = HUB_DEV * slots + (rows - HUB_DEV) * HALF
    local = near[0].shape[2]
    return pl.pallas_call(
        first_image_kernel,
        out_shape=image_shapes(near)
        + (
            jax.ShapeDtypeStruct((total,), jnp.int32),
            jax.ShapeDtypeStruct((total, bs // part_count, bs), F32),
        ),
        in_specs=[SMEM, SMEM, SMEM] + [ANY] * 8,
        out_specs=(VMEM, VMEM, SMEM, VMEM),
        scratch_shapes=[
            pltpu.SMEM((rows,), jnp.int32),
            pltpu.SMEM((rows * (SIDE * SIDE + 2),), jnp.int32),
            pltpu.VMEM((table_rows(near, hubs), local), BF),
            pltpu.VMEM((total, bs, bs), F32),
            pltpu.SemaphoreType.DMA,
            pltpu.SemaphoreType.DMA,
        ],
        name="image_first",
    )(counts, pattern, ids, omega, *near, *hubs)


def later_image(counts, lookup, mine, partner, near, hubs):
    total = lookup.shape[0]
    bs = mine.shape[3]
    local = near[0].shape[2]
    return pl.pallas_call(
        later_image_kernel,
        out_shape=image_shapes(near),
        in_specs=[SMEM, SMEM] + [ANY] * 9,
        out_specs=(VMEM, VMEM),
        scratch_shapes=[
            pltpu.SMEM(counts.shape, jnp.int32),
            pltpu.VMEM((table_rows(near, hubs), local), BF),
            pltpu.VMEM((total, bs, bs), F32),
            pltpu.SemaphoreType.DMA,
            pltpu.SemaphoreType.DMA,
        ],
        name="image_later",
    )(counts, lookup, mine, partner, *near, *hubs)


def gradient_kernel(scale, *refs):
    lookup = refs[0]
    x_near, x_hubs, m_near, m_hubs = refs[1:4], refs[4:8], refs[8:11], refs[11:15]
    keep, send = refs[15:17]
    x_table, m_table, sem = refs[17:]
    plain, bs, _ = x_near[0].shape
    rows = plain + HUB_DEV
    slots = (lookup.shape[0] - plain * HALF) // HUB_DEV
    moves = table_copies(x_near, x_hubs, x_table, sem) + table_copies(m_near, m_hubs, m_table, sem)
    for move in moves:
        move.start()
    for move in moves:
        move.wait()
    part = lax.axis_index("samp")
    y, core = part // CORES, part % CORES
    share = keep.shape[2]

    def group(start, own):
        mine = aligned(own, bs)
        left = jnp.concatenate([m_table[mine, :], x_table[mine, :]], axis=1)
        right = []
        for k in range(GROUP):
            at = aligned(lookup[start + k], bs)
            right.append(jnp.concatenate([x_table[at, :], m_table[at, :]], axis=1))
        both = lax.dot_general(
            left,
            jnp.concatenate(right, axis=0),
            (((1,), (1,)), ((), ())),
            preferred_element_type=F32,
        )
        both = both * scale
        for k in range(GROUP):
            tile = both[:, k * bs : (k + 1) * bs].reshape(SIDE, CORES, share, bs)
            even, odd = tile[:, 0], tile[:, 1]
            stay = jnp.where(core == 0, even, odd)
            leave = jnp.where(core == 0, odd, even)
            for g in range(SIDE):
                to = (g + SIDE - y) % SIDE
                keep[to, start + k] = stay[g]
                send[to, start + k] = leave[g].astype(send.dtype)

    for p in range(HUB_DEV):
        group(p * slots, 3 * plain + p)
        group(p * slots + GROUP, 3 * plain + p)

    def step(p, _):
        group(HUB_DEV * slots + p * HALF, plain + p)
        return 0

    lax.fori_loop(0, rows - HUB_DEV, step, 0)


def gradient(lookup, x_near, x_hubs, m_near, m_hubs, scale, part_count):
    total = lookup.shape[0]
    bs = x_near[0].shape[1]
    local = x_near[0].shape[2]
    shape = (SIDE, total, bs // part_count, bs)
    table = pltpu.VMEM((table_rows(x_near, x_hubs), local), BF)
    return pl.pallas_call(
        lambda *refs: gradient_kernel(scale, *refs),
        out_shape=(jax.ShapeDtypeStruct(shape, F32), jax.ShapeDtypeStruct(shape, F32)),
        in_specs=[SMEM] + [ANY] * 14,
        out_specs=(VMEM, VMEM),
        scratch_shapes=[table, table, pltpu.SemaphoreType.DMA],
        name="gradient",
    )(lookup, *x_near, *x_hubs, *m_near, *m_hubs)


def add_kernel(keep, other, own, *sends):
    own[...] = keep[0] + other[0]
    for j, ref in enumerate(sends):
        ref[...] = (keep[j + 1] + other[j + 1]).astype(ref.dtype)


def add_cores(keep, other):
    side, total, share, bs = keep.shape
    block = total // 4
    wide = pl.BlockSpec((side, block, share, bs), lambda i: (0, i, 0, 0))
    flat = pl.BlockSpec((block, share, bs), lambda i: (i, 0, 0))
    return pl.pallas_call(
        add_kernel,
        grid=(4,),
        out_shape=tuple(jax.ShapeDtypeStruct((total, share, bs), F32) for _ in range(side)),
        in_specs=[wide, wide],
        out_specs=(flat,) * side,
        name="add_cores",
    )(keep, other)


def new_tile(tile, slope, leading, live, part, share):
    stepped = tile - STEP_SIZE * slope
    edge = STEP_SIZE * PENALTY
    shrunk = stepped - jnp.minimum(jnp.maximum(stepped, -edge), edge)
    if leading:
        shape = stepped.shape
        row = part * share + lax.broadcasted_iota(jnp.int32, shape, 0)
        col = lax.broadcasted_iota(jnp.int32, shape, 1)
        barrier = 0.5 * (stepped + jnp.sqrt(stepped * stepped + 4.0 * STEP_SIZE))
        shrunk = jnp.where(row == col, barrier, shrunk)
    return jnp.where(live, shrunk, 0.0)


def prox_kernel(last, slots, counts, tiles, own, a, b, c, out, order):
    rows = order.shape[0]
    row_order(counts, order, slots)
    part = lax.axis_index("samp")
    share = own.shape[1]

    def slot(row, s, k, n):
        slope = (own[s] + a[s]) + (b[s] + c[s])
        value = new_tile(tiles[s], slope, k == 0, k < n, part, share)
        if last:
            out[row, k] = value
        else:
            out[s] = value

    for p in range(HUB_DEV):
        for k in range(slots):
            slot(order[p], p * slots + k, k, slots)

    def plain(p, _):
        row = order[HUB_DEV + p]
        n = counts[row]
        for k in range(HALF):
            slot(row, HUB_DEV * slots + p * HALF + k, k, n)
        if last:
            for k in range(HALF, slots):
                out[row, k] = jnp.zeros(out.shape[2:], F32)
        return 0

    lax.fori_loop(0, rows - HUB_DEV, plain, 0)


def prox(counts, tiles, terms, slots, last):
    rows = counts.shape[0]
    total, share, bs = tiles.shape
    shape = (rows, slots, share, bs) if last else (total, share, bs)
    return pl.pallas_call(
        lambda *refs: prox_kernel(last, slots, *refs),
        out_shape=jax.ShapeDtypeStruct(shape, F32),
        in_specs=[SMEM] + [VMEM] * 5,
        out_specs=VMEM,
        scratch_shapes=[pltpu.SMEM((rows,), jnp.int32)],
        name="prox_last" if last else "prox",
    )(counts, tiles, *terms)


def share_near(value):
    size = lax.axis_size("var")
    up = [(i, i + 1) for i in range(size - 1)]
    down = [(i + 1, i) for i in range(size - 1)]
    return lax.ppermute(value, "var", up), value, lax.ppermute(value, "var", down)


def share_hubs(value):
    by_z = [value] + [lax.ppermute(value, "var", var_shift(0, d)) for d in (1, -1, 2)]
    column = jnp.stack(by_z)
    return [column] + [lax.ppermute(column, "var", var_shift(d, 0)) for d in (1, -1, 2)]


def per_device(data, omega, pattern, counts):
    parts = lax.axis_size("samp")
    rows, slots, bs, _ = omega.shape
    scale = 0.5 / (data.shape[0] * parts)
    x_own, x_hub = pack(data, counts, slots, bs)
    x_near = share_near(x_own)
    x_hubs = share_hubs(x_hub)
    ids = jnp.stack([g[:, HUB_DEV * bs : HUB_DEV * bs + HUB_DEV, 0] for g in x_hubs])
    ids = ids.reshape(-1).astype(jnp.int32)
    for iteration in range(ITERS):
        if iteration == 0:
            m_own, m_hub, lookup, tiles = first_image(
                counts, pattern, ids, omega, x_near, x_hubs, parts
            )
        else:
            around = [
                tiles,
                lax.ppermute(tiles, "samp", samp_shift(-1, 0)),
                lax.ppermute(tiles, "samp", samp_shift(2, 0)),
                lax.ppermute(tiles, "samp", samp_shift(1, 0)),
            ]
            mine = jnp.stack(around)
            partner = lax.ppermute(mine, "samp", samp_shift(0, 1))
            m_own, m_hub = later_image(counts, lookup, mine, partner, x_near, x_hubs)
        m_near = share_near(m_own)
        m_hubs = share_hubs(m_hub)
        keep, send = gradient(lookup, x_near, x_hubs, m_near, m_hubs, scale, parts)
        other = lax.ppermute(send, "samp", samp_shift(0, 1))
        own, up, across, down = add_cores(keep, other)
        terms = (
            own,
            lax.ppermute(up, "samp", samp_shift(1, 0)),
            lax.ppermute(across, "samp", samp_shift(2, 0)),
            lax.ppermute(down, "samp", samp_shift(-1, 0)),
        )
        tiles = prox(counts, tiles, terms, slots, iteration == ITERS - 1)
    return tiles


def solution(mesh):
    placed = (P("samp", "var"), P("var", None, None, None), P("var", None), P("var"))
    return jax.shard_map(
        per_device,
        mesh=mesh,
        in_specs=placed,
        out_specs=P("var", None, "samp", None),
        check_vma=False,
    )
```

```python
import jax
import jax.numpy as jnp
from jax import lax
from jax.experimental import pallas as pl
from jax.experimental.pallas import tpu as pltpu
from jax.sharding import PartitionSpec as P

HUB_DEV = 2
ITERS = 2
STEP_SIZE = 0.25
PENALTY = 1.0
HALF = 4
GROUP = 4
SIDE = 4
CORES = 2
LEVELS = 32000.0
TINY = 1e-30
BF = jnp.bfloat16
F32 = jnp.float32
WIRE = jnp.int16
ANY = pl.BlockSpec(memory_space=pl.ANY)
SMEM = pl.BlockSpec(memory_space=pltpu.SMEM)
VMEM = pl.BlockSpec(memory_space=pltpu.VMEM)


def grant(mib):
    return pltpu.CompilerParams(vmem_limit_bytes=mib << 20)


def cost(flops, moved):
    return pl.CostEstimate(flops=flops, bytes_accessed=moved, transcendentals=0)


def var_shift(dx, dz):
    return [
        (x * SIDE + z, ((x + dx) % SIDE) * SIDE + (z + dz) % SIDE)
        for x in range(SIDE)
        for z in range(SIDE)
    ]


def samp_shift(dy, dc):
    return [
        (y * CORES + c, ((y + dy) % SIDE) * CORES + (c + dc) % CORES)
        for y in range(SIDE)
        for c in range(CORES)
    ]


def row_order(counts, order, slots):
    def step(r, carry):
        hubs, others = carry
        hub = jnp.where(counts[r] == slots, 1, 0)
        order[jnp.where(hub == 1, hubs, HUB_DEV + others)] = r
        return hubs + hub, others + 1 - hub

    lax.fori_loop(0, order.shape[0], step, (jnp.int32(0), jnp.int32(0)))


def slot_base(p, slots):
    return p * slots if p < HUB_DEV else HUB_DEV * slots + (p - HUB_DEV) * HALF


def aligned(index, size):
    return pl.ds(pl.multiple_of(index * size, size), size)


def turned(data, row, bs):
    shape = (bs, bs)
    eye = lax.broadcasted_iota(jnp.int32, shape, 0) == lax.broadcasted_iota(jnp.int32, shape, 1)
    block = data[:, aligned(row, bs)]
    return lax.dot_general(
        eye.astype(F32).astype(BF), block, (((1,), (1,)), ((), ())), preferred_element_type=F32
    ).astype(BF)


def pack_hub_kernel(slots, bs, counts, data, out, order):
    row_order(counts, order, slots)
    first = lax.axis_index("var") * order.shape[0]
    for p in range(HUB_DEV):
        out[p * bs : (p + 1) * bs, :] = turned(data, order[p], bs)
    tail = out.shape[0] - HUB_DEV * bs
    lead = lax.broadcasted_iota(jnp.int32, (tail, out.shape[1]), 0) == 0
    ids = jnp.where(lead, first + order[0], first + order[1])
    out[HUB_DEV * bs :, :] = ids.astype(F32).astype(BF)


def pack_plain_kernel(slots, bs, counts, data, _, out, order):
    row_order(counts, order, slots)
    for p in range(out.shape[0]):
        out[p] = turned(data, order[HUB_DEV + p], bs)


def pack_hub(data, counts, slots, bs):
    return pl.pallas_call(
        lambda *refs: pack_hub_kernel(slots, bs, *refs),
        out_shape=jax.ShapeDtypeStruct((HUB_DEV * bs + 16, data.shape[0]), BF),
        in_specs=[SMEM, VMEM],
        out_specs=VMEM,
        scratch_shapes=[pltpu.SMEM(counts.shape, jnp.int32)],
        compiler_params=grant(8),
        cost_estimate=cost(1 << 20, 1 << 20),
        name="pack_hub",
    )(counts, data)


def pack_plain(data, counts, slots, bs, after):
    return pl.pallas_call(
        lambda *refs: pack_plain_kernel(slots, bs, *refs),
        out_shape=jax.ShapeDtypeStruct((counts.shape[0] - HUB_DEV, bs, data.shape[0]), BF),
        in_specs=[SMEM, VMEM, ANY],
        out_specs=VMEM,
        scratch_shapes=[pltpu.SMEM(counts.shape, jnp.int32)],
        compiler_params=grant(8),
        cost_estimate=cost(1 << 20, 1 << 20),
        name="pack_plain",
    )(counts, data, after)


class Gather:
    def __init__(self, near, hubs, table, sem, bs):
        below, below_edge, own, above, above_edge = near
        plain = own.shape[0]
        size = plain * bs
        z = lax.axis_index("var") % SIDE

        def copy(ref, at):
            return pltpu.make_async_copy(ref.reshape(size, ref.shape[2]), table.at[pl.ds(at, size), :], sem)

        self.choices = [
            (z == 0, copy(below, 0), copy(below_edge, 0)),
            (z == SIDE - 1, copy(above, 2 * size), copy(above_edge, 2 * size)),
        ]
        self.copies = [copy(own, size)]
        at = 3 * size
        for ref in hubs:
            for i in range(ref.shape[0]):
                self.copies.append(
                    pltpu.make_async_copy(
                        ref.at[i, pl.ds(0, HUB_DEV * bs), :],
                        table.at[pl.ds(at, HUB_DEV * bs), :],
                        sem,
                    )
                )
                at += HUB_DEV * bs

    def start(self):
        for copy in self.copies:
            copy.start()
        for edge, usual, other in self.choices:
            pl.when(edge)(other.start)
            pl.when(jnp.logical_not(edge))(usual.start)

    def wait(self):
        for copy in self.copies:
            copy.wait()
        for _, usual, _ in self.choices:
            usual.wait()


def fill_lookup(pattern, ids, order, inverse, lookup):
    rows, slots = pattern.shape
    plain = rows - HUB_DEV
    base = lax.axis_index("var") * rows

    def clear(i, _):
        inverse[base + i] = -1
        return 0

    lax.fori_loop(0, 3 * rows, clear, 0)

    def mark(q, _):
        inverse[ids[q] + rows] = 3 * plain + q
        return 0

    lax.fori_loop(0, ids.shape[0], mark, 0)
    for side in range(3):

        def place(i, found):
            at = base + side * rows + i
            seen = inverse[at]
            inverse[at] = jnp.where(seen < 0, side * plain + found, seen)
            return found + jnp.where(seen < 0, 1, 0)

        lax.fori_loop(0, rows, place, jnp.int32(0))
    total = 3 * plain + ids.shape[0]
    for p in range(rows):
        for k in range(slots if p < HUB_DEV else HALF):
            c = inverse[pattern[order[p], k] + rows]
            lookup[slot_base(p, slots) + k] = jnp.clip(c, 0, total - 1)


def image_group(tile_of, blocks_of, live, bs):
    high, low, blocks = [], [], []
    for k in range(GROUP):
        tile = tile_of(k)
        if live is not None:
            tile = jnp.where(k < live, tile, 0.0)
        top = tile.astype(BF)
        high.append(top)
        low.append((tile - top.astype(F32)).astype(BF))
        blocks.append(blocks_of(k))
    left = jnp.concatenate([jnp.concatenate(high, axis=1), jnp.concatenate(low, axis=1)], axis=0)
    both = jnp.dot(left, jnp.concatenate(blocks, axis=0), preferred_element_type=F32)
    return both[:bs] + both[bs:]


def hub_images(tile_of, lookup, table, out, slots, bs):
    for p in range(HUB_DEV):
        total = None
        for start in range(p * slots, (p + 1) * slots, GROUP):
            part = image_group(
                lambda k: tile_of(start + k),
                lambda k: table[aligned(lookup[start + k], bs), :],
                None,
                bs,
            )
            total = part if total is None else total + part
        out[p * bs : (p + 1) * bs, :] = total.astype(BF)


def plain_images(counts, order, ready, tile_of, lookup, table, out, slots, bs):
    def one(p, _):
        ready(p)
        start = HUB_DEV * slots + p * HALF
        image = image_group(
            lambda k: tile_of(p * HALF + k),
            lambda k: table[aligned(lookup[start + k], bs), :],
            counts[order[HUB_DEV + p]],
            bs,
        )
        out[p] = image.astype(BF)
        return 0

    lax.fori_loop(0, out.shape[0], one, 0, unroll=2)


def first_hub_kernel(*refs):
    counts, pattern, ids, omega = refs[:4]
    near, hubs = refs[4:9], refs[9:13]
    out, lookup, table, rows_out = refs[13:17]
    order, inverse, tiles, table_sem, tile_sem = refs[17:]
    rows, slots = pattern.shape
    bs, share = tiles.shape[1], rows_out.shape[1]
    row_order(counts, order, slots)
    gather = Gather(near, hubs, table, table_sem, bs)
    gather.start()
    part = aligned(lax.axis_index("samp"), share)
    moves = []
    for p in range(rows):
        n = slots if p < HUB_DEV else HALF
        at = pl.ds(slot_base(p, slots), n)
        moves.append(
            pltpu.make_async_copy(omega.at[order[p], pl.ds(0, n), part], rows_out.at[at], tile_sem)
        )
        if p < HUB_DEV:
            moves.append(pltpu.make_async_copy(omega.at[order[p]], tiles.at[at], tile_sem))
    for move in moves:
        move.start()
    fill_lookup(pattern, ids, order, inverse, lookup)
    for move in moves:
        move.wait()
    gather.wait()
    hub_images(lambda s: tiles[s], lookup, table, out, slots, bs)


def first_hub(counts, pattern, ids, omega, near, hubs, part_count):
    rows, slots, bs, _ = omega.shape
    total = HUB_DEV * slots + (rows - HUB_DEV) * HALF
    local = hubs[0].shape[2]
    table = (3 * (rows - HUB_DEV) + SIDE * SIDE * HUB_DEV) * bs
    return pl.pallas_call(
        first_hub_kernel,
        out_shape=(
            jax.ShapeDtypeStruct((HUB_DEV * bs, local), BF),
            jax.ShapeDtypeStruct((total,), jnp.int32),
            jax.ShapeDtypeStruct((table, local), BF),
            jax.ShapeDtypeStruct((total, bs // part_count, bs), F32),
        ),
        in_specs=[SMEM, SMEM, SMEM] + [ANY] * 10,
        out_specs=(VMEM, SMEM, VMEM, VMEM),
        scratch_shapes=[
            pltpu.SMEM((rows,), jnp.int32),
            pltpu.SMEM((rows * (SIDE * SIDE + 2),), jnp.int32),
            pltpu.VMEM((HUB_DEV * slots, bs, bs), F32),
            pltpu.SemaphoreType.DMA,
            pltpu.SemaphoreType.DMA,
        ],
        compiler_params=grant(16),
        cost_estimate=cost(1 << 28, 12 << 20),
        name="hub_first",
    )(counts, pattern, ids, omega, *near, *hubs)


def first_plain_kernel(slots, *refs):
    counts, lookup, omega, table, _, out = refs[:6]
    order, tiles, sems = refs[6:]
    bs = tiles.shape[1]
    row_order(counts, order, slots)

    def move(p):
        return pltpu.make_async_copy(
            omega.at[order[HUB_DEV + p], pl.ds(0, HALF)], tiles.at[pl.ds(p * HALF, HALF)], sems.at[p]
        )

    for p in range(out.shape[0]):
        move(p).start()
    plain_images(
        counts, order, lambda p: move(p).wait(), lambda s: tiles[s], lookup, table, out, slots, bs
    )


def first_plain(counts, lookup, omega, table, after):
    rows, slots, bs, _ = omega.shape
    plain = rows - HUB_DEV
    return pl.pallas_call(
        lambda *refs: first_plain_kernel(slots, *refs),
        out_shape=jax.ShapeDtypeStruct((plain, bs, table.shape[1]), BF),
        in_specs=[SMEM, SMEM, ANY, VMEM, ANY],
        out_specs=VMEM,
        scratch_shapes=[
            pltpu.SMEM((rows,), jnp.int32),
            pltpu.VMEM((plain * HALF, bs, bs), F32),
            pltpu.SemaphoreType.DMA((plain,)),
        ],
        compiler_params=grant(16),
        cost_estimate=cost(1 << 29, 10 << 20),
        name="plain_first",
    )(counts, lookup, omega, table, after)


def wire_scales(tail, scales):
    exponent = tail.astype(jnp.int32).astype(F32).reshape(scales.shape)
    scales[...] = jnp.exp2(exponent) * (1.0 / LEVELS)


def to_wire(read, out, scales, total):
    scales[...] = jnp.ones_like(scales)

    def peak(s, _):
        scales[pl.ds(s, 1), :] = jnp.max(jnp.abs(read(s)), axis=0, keepdims=True)
        return 0

    lax.fori_loop(0, total, peak, 0, unroll=8)
    exponent = jnp.ceil(jnp.log2(jnp.maximum(scales[...], TINY)))
    tail = exponent.reshape(-1, *out.shape[1:])
    out[total:] = tail.astype(jnp.int32).astype(WIRE)
    scales[...] = jnp.exp2(-exponent) * LEVELS

    def put(s, _):
        out[s] = jnp.round(read(s) * scales[pl.ds(s, 1), :]).astype(jnp.int32).astype(WIRE)
        return 0

    lax.fori_loop(0, total, put, 0, unroll=8)


def wire_shape(total, share, bs):
    return (total + -(-total // share), share, bs)


def later_image_kernel(slots, *refs):
    counts, lookup, mine, partner, table, hub_out, out = refs[:7]
    order, levels, tails, scales, sem = refs[7:]
    total, bs = lookup.shape[0], levels.shape[1]
    share = mine.shape[2]
    row_order(counts, order, slots)
    part = lax.axis_index("samp")
    moves = []
    for j in range(SIDE):
        for ref, core in ((mine, part % CORES), (partner, (part + 1) % CORES)):
            at = ((part // CORES + j) % SIDE) * CORES + core
            moves.append(
                pltpu.make_async_copy(
                    ref.at[j, pl.ds(0, total)], levels.at[:, aligned(at, share), :], sem
                )
            )
            moves.append(
                pltpu.make_async_copy(
                    ref.at[j, pl.ds(total, mine.shape[1] - total)], tails.at[at], sem
                )
            )
    for move in moves:
        move.start()
    for move in moves:
        move.wait()
    for g in range(SIDE * CORES):
        wire_scales(tails[g], scales.at[g])

    def tile_of(s):
        rows = [
            levels[s, g * share : (g + 1) * share, :].astype(jnp.int32).astype(F32)
            * scales[g, pl.ds(s, 1), :]
            for g in range(SIDE * CORES)
        ]
        return jnp.concatenate(rows, axis=0)

    hub_images(tile_of, lookup, table, hub_out, slots, bs)
    start = HUB_DEV * slots
    plain_images(
        counts, order, lambda p: None, lambda s: tile_of(start + s), lookup, table, out, slots, bs
    )


def later_image(counts, lookup, mine, partner, table, slots):
    total = lookup.shape[0]
    rows = counts.shape[0]
    _, long, share, bs = mine.shape
    local = table.shape[1]
    groups = SIDE * CORES
    return pl.pallas_call(
        lambda *refs: later_image_kernel(slots, *refs),
        out_shape=(
            jax.ShapeDtypeStruct((HUB_DEV * bs, local), BF),
            jax.ShapeDtypeStruct((rows - HUB_DEV, bs, local), BF),
        ),
        in_specs=[SMEM, SMEM, ANY, ANY, VMEM],
        out_specs=(VMEM, VMEM),
        scratch_shapes=[
            pltpu.SMEM(counts.shape, jnp.int32),
            pltpu.VMEM((total, bs, bs), WIRE),
            pltpu.VMEM((groups, long - total, share, bs), WIRE),
            pltpu.VMEM((groups, (long - total) * share, bs), F32),
            pltpu.SemaphoreType.DMA,
        ],
        compiler_params=grant(16),
        cost_estimate=cost(1 << 29, 10 << 20),
        name="image_later",
    )(counts, lookup, mine, partner, table)


def gradient_kernel(scale, slots, *refs):
    lookup, x_table = refs[:2]
    near, hubs = refs[2:7], refs[7:11]
    keep, send, m_table, sem = refs[11:]
    plain, bs, _ = near[0].shape
    gather = Gather(near, hubs, m_table, sem, bs)
    gather.start()
    gather.wait()
    part = lax.axis_index("samp")
    y, core = part // CORES, part % CORES
    share = keep.shape[2]

    def group(start, own):
        mine = aligned(own, bs)
        left = jnp.concatenate([m_table[mine, :], x_table[mine, :]], axis=1)
        right = []
        for k in range(GROUP):
            at = aligned(lookup[start + k], bs)
            right.append(jnp.concatenate([x_table[at, :], m_table[at, :]], axis=1))
        both = lax.dot_general(
            left,
            jnp.concatenate(right, axis=0),
            (((1,), (1,)), ((), ())),
            preferred_element_type=F32,
        )
        both = both * scale
        for k in range(GROUP):
            tile = both[:, k * bs : (k + 1) * bs].reshape(SIDE, CORES, share, bs)
            even, odd = tile[:, 0], tile[:, 1]
            stay = jnp.where(core == 0, even, odd)
            leave = jnp.where(core == 0, odd, even)
            for g in range(SIDE):
                to = (g + SIDE - y) % SIDE
                keep[to, start + k] = stay[g]
                send[to, start + k] = leave[g]

    for p in range(HUB_DEV):
        for start in range(p * slots, (p + 1) * slots, GROUP):
            group(start, 3 * plain + p)

    def step(p, _):
        group(HUB_DEV * slots + p * HALF, plain + p)
        return 0

    lax.fori_loop(0, plain, step, 0, unroll=2)


def gradient(lookup, table, near, hubs, scale, slots, part_count):
    total = lookup.shape[0]
    bs = near[0].shape[1]
    shape = jax.ShapeDtypeStruct((SIDE, total, bs // part_count, bs), F32)
    return pl.pallas_call(
        lambda *refs: gradient_kernel(scale, slots, *refs),
        out_shape=(shape, shape),
        in_specs=[SMEM, VMEM] + [ANY] * 9,
        out_specs=(VMEM, VMEM),
        scratch_shapes=[pltpu.VMEM(table.shape, BF), pltpu.SemaphoreType.DMA],
        compiler_params=grant(24),
        cost_estimate=cost(1 << 30, 16 << 20),
        name="gradient",
    )(lookup, table, *near, *hubs)


def add_kernel(keep, other, own, *refs):
    sends, total_sum, scales = refs[:-2], refs[-2], refs[-1]
    total = own.shape[0]
    own[...] = keep[0] + other[0]
    for j, ref in enumerate(sends):
        total_sum[...] = keep[j + 1] + other[j + 1]
        to_wire(lambda s: total_sum[s], ref, scales, total)


def add_cores(keep, other):
    side, total, share, bs = keep.shape
    wire = jax.ShapeDtypeStruct(wire_shape(total, share, bs), WIRE)
    return pl.pallas_call(
        add_kernel,
        out_shape=(jax.ShapeDtypeStruct((total, share, bs), F32),) + (wire,) * (side - 1),
        in_specs=[VMEM, VMEM],
        out_specs=(VMEM,) * side,
        scratch_shapes=[
            pltpu.VMEM((total, share, bs), F32),
            pltpu.VMEM(((wire.shape[0] - total) * share, bs), F32),
        ],
        compiler_params=grant(16),
        name="add_cores",
    )(keep, other)


def new_tile(tile, slope, leading, live, part, share):
    stepped = tile - STEP_SIZE * slope
    edge = STEP_SIZE * PENALTY
    shrunk = stepped - jnp.minimum(jnp.maximum(stepped, -edge), edge)
    if leading:
        shape = stepped.shape
        row = part * share + lax.broadcasted_iota(jnp.int32, shape, 0)
        col = lax.broadcasted_iota(jnp.int32, shape, 1)
        barrier = 0.5 * (stepped + jnp.sqrt(stepped * stepped + 4.0 * STEP_SIZE))
        shrunk = jnp.where(row == col, barrier, shrunk)
    return jnp.where(live, shrunk, 0.0)


def prox_kernel(last, slots, counts, tiles, own, *refs):
    sends = refs[: SIDE - 1]
    outs = refs[SIDE - 1 : -2]
    order, scales = refs[-2:]
    rows = order.shape[0]
    row_order(counts, order, slots)
    part = lax.axis_index("samp")
    total, share, bs = own.shape
    for j, ref in enumerate(sends):
        wire_scales(ref[total:], scales.at[j])

    def slot(row, s, k, n):
        slope = own[s]
        for j, ref in enumerate(sends):
            slope = slope + ref[s].astype(jnp.int32).astype(F32) * scales[j, pl.ds(s, 1), :]
        value = new_tile(tiles[s], slope, k == 0, k < n, part, share)
        if last:
            outs[0][row, k] = value
        else:
            outs[0][s] = value

    for p in range(HUB_DEV):
        for k in range(slots):
            slot(order[p], p * slots + k, k, slots)

    def plain(p, _):
        row = order[HUB_DEV + p]
        n = counts[row]
        for k in range(HALF):
            slot(row, HUB_DEV * slots + p * HALF + k, k, n)
        if last:
            for k in range(HALF, slots):
                outs[0][row, k] = jnp.zeros((share, bs), F32)
        return 0

    lax.fori_loop(0, rows - HUB_DEV, plain, 0, unroll=2)
    if not last:
        to_wire(lambda s: outs[0][s], outs[1], scales.at[0], total)


def prox(counts, tiles, terms, slots, last):
    rows = counts.shape[0]
    total, share, bs = tiles.shape
    wire = wire_shape(total, share, bs)
    if last:
        outs = (jax.ShapeDtypeStruct((rows, slots, share, bs), F32),)
    else:
        outs = (jax.ShapeDtypeStruct((total, share, bs), F32), jax.ShapeDtypeStruct(wire, WIRE))
    return pl.pallas_call(
        lambda *refs: prox_kernel(last, slots, *refs),
        out_shape=outs,
        in_specs=[SMEM] + [VMEM] * 5,
        out_specs=(VMEM,) * len(outs),
        scratch_shapes=[
            pltpu.SMEM((rows,), jnp.int32),
            pltpu.VMEM((SIDE - 1, (wire[0] - total) * share, bs), F32),
        ],
        compiler_params=grant(16),
        name="prox_last" if last else "prox",
    )(counts, tiles, *terms)


def share_near(value):
    size = lax.axis_size("var")
    up = [(i, i + 1) for i in range(size - 1)]
    moves = []
    for pairs in (up, [(j, i) for i, j in up]):
        inner = [(i, j) for i, j in pairs if i // SIDE == j // SIDE]
        edge = [(i, j) for i, j in pairs if i // SIDE != j // SIDE]
        moves.append((lax.ppermute(value, "var", edge), lax.ppermute(value, "var", inner)))
    (below_edge, below), (above_edge, above) = moves
    return below, below_edge, value, above, above_edge


def share_hubs(value):
    by_z = [value] + [lax.ppermute(value, "var", var_shift(0, d)) for d in (1, -1, 2)]
    column = jnp.stack(by_z)
    return [column] + [lax.ppermute(column, "var", var_shift(d, 0)) for d in (1, -1, 2)]


def per_device(data, omega, pattern, counts):
    parts = lax.axis_size("samp")
    rows, slots, bs, _ = omega.shape
    scale = 0.5 / (data.shape[0] * parts)
    x_hub = pack_hub(data, counts, slots, bs)
    x_hubs = share_hubs(x_hub)
    x_near = share_near(pack_plain(data, counts, slots, bs, x_hub))
    ids = jnp.stack([g[:, HUB_DEV * bs : HUB_DEV * bs + HUB_DEV, 0] for g in x_hubs])
    ids = ids.reshape(-1).astype(jnp.int32)
    for iteration in range(ITERS):
        if iteration == 0:
            m_hub, lookup, table, tiles = first_hub(
                counts, pattern, ids, omega, x_near, x_hubs, parts
            )
            m_own = first_plain(counts, lookup, omega, table, m_hub)
        else:
            mine = jnp.stack(
                [
                    sent,
                    lax.ppermute(sent, "samp", samp_shift(-1, 0)),
                    lax.ppermute(sent, "samp", samp_shift(2, 0)),
                    lax.ppermute(sent, "samp", samp_shift(1, 0)),
                ]
            )
            partner = lax.ppermute(mine, "samp", samp_shift(0, 1))
            m_hub, m_own = later_image(counts, lookup, mine, partner, table, slots)
        m_hubs = share_hubs(m_hub)
        m_near = share_near(m_own)
        keep, leave = gradient(lookup, table, m_near, m_hubs, scale, slots, parts)
        other = lax.ppermute(leave, "samp", samp_shift(0, 1))
        own, up, across, down = add_cores(keep, other)
        terms = (
            own,
            lax.ppermute(up, "samp", samp_shift(1, 0)),
            lax.ppermute(across, "samp", samp_shift(2, 0)),
            lax.ppermute(down, "samp", samp_shift(-1, 0)),
        )
        if iteration < ITERS - 1:
            tiles, sent = prox(counts, tiles, terms, slots, False)
        else:
            (tiles,) = prox(counts, tiles, terms, slots, True)
    return tiles


def solution(mesh):
    placed = (P("samp", "var"), P("var", None, None, None), P("var", None), P("var"))
    return jax.shard_map(
        per_device,
        mesh=mesh,
        in_specs=placed,
        out_specs=P("var", None, "samp", None),
        check_vma=False,
    )
```

```python
import jax
import jax.numpy as jnp
from jax import lax
from jax.experimental import pallas as pl
from jax.experimental.pallas import tpu as pltpu
from jax.sharding import PartitionSpec as P


HUB_DEV = 2
ITERS = 2
STEP_SIZE = 0.25
PENALTY = 1.0
HALF = 4
GROUP = 4
SIDE = 4
CORES = 2
LEVELS = 32000.0
TINY = 1e-30
BF = jnp.bfloat16
F32 = jnp.float32
WIRE = jnp.int16
ANY = pl.BlockSpec(memory_space=pl.ANY)
SMEM = pl.BlockSpec(memory_space=pltpu.SMEM)
VMEM = pl.BlockSpec(memory_space=pltpu.VMEM)


def grant(mib):
    return pltpu.CompilerParams(vmem_limit_bytes=mib << 20)


def cost(flops, moved):
    return pl.CostEstimate(flops=flops, bytes_accessed=moved, transcendentals=0)


def var_shift(dx, dz):
    return [
        (x * SIDE + z, ((x + dx) % SIDE) * SIDE + (z + dz) % SIDE)
        for x in range(SIDE)
        for z in range(SIDE)
    ]


def samp_shift(dy, dc):
    return [
        (y * CORES + c, ((y + dy) % SIDE) * CORES + (c + dc) % CORES)
        for y in range(SIDE)
        for c in range(CORES)
    ]


def row_order(counts, order, slots):
    def step(r, carry):
        hubs, others = carry
        hub = jnp.where(counts[r] == slots, 1, 0)
        order[jnp.where(hub == 1, hubs, HUB_DEV + others)] = r
        return hubs + hub, others + 1 - hub

    lax.fori_loop(0, order.shape[0], step, (jnp.int32(0), jnp.int32(0)))


def slot_base(p, slots):
    return p * slots if p < HUB_DEV else HUB_DEV * slots + (p - HUB_DEV) * HALF


def aligned(index, size):
    return pl.ds(pl.multiple_of(index * size, size), size)


def turned(data, row, bs):
    shape = (bs, bs)
    eye = lax.broadcasted_iota(jnp.int32, shape, 0) == lax.broadcasted_iota(jnp.int32, shape, 1)
    block = data[:, aligned(row, bs)]
    return lax.dot_general(
        eye.astype(F32).astype(BF), block, (((1,), (1,)), ((), ())), preferred_element_type=F32
    ).astype(BF)


def pack_hub_kernel(slots, bs, counts, data, out, order):
    row_order(counts, order, slots)
    first = lax.axis_index("var") * order.shape[0]
    for p in range(HUB_DEV):
        out[p * bs : (p + 1) * bs, :] = turned(data, order[p], bs)
    tail = out.shape[0] - HUB_DEV * bs
    lead = lax.broadcasted_iota(jnp.int32, (tail, out.shape[1]), 0) == 0
    ids = jnp.where(lead, first + order[0], first + order[1])
    out[HUB_DEV * bs :, :] = ids.astype(F32).astype(BF)


def pack_plain_kernel(slots, bs, counts, data, _, out, order):
    row_order(counts, order, slots)
    for p in range(out.shape[0]):
        out[p] = turned(data, order[HUB_DEV + p], bs)


def pack_hub(data, counts, slots, bs):
    return pl.pallas_call(
        lambda *refs: pack_hub_kernel(slots, bs, *refs),
        out_shape=jax.ShapeDtypeStruct((HUB_DEV * bs + 16, data.shape[0]), BF),
        in_specs=[SMEM, VMEM],
        out_specs=VMEM,
        scratch_shapes=[pltpu.SMEM(counts.shape, jnp.int32)],
        compiler_params=grant(8),
        cost_estimate=cost(1 << 20, 1 << 20),
        name="pack_hub",
    )(counts, data)


def pack_plain(data, counts, slots, bs, after):
    return pl.pallas_call(
        lambda *refs: pack_plain_kernel(slots, bs, *refs),
        out_shape=jax.ShapeDtypeStruct((counts.shape[0] - HUB_DEV, bs, data.shape[0]), BF),
        in_specs=[SMEM, VMEM, ANY],
        out_specs=VMEM,
        scratch_shapes=[pltpu.SMEM(counts.shape, jnp.int32)],
        compiler_params=grant(8),
        cost_estimate=cost(1 << 20, 1 << 20),
        name="pack_plain",
    )(counts, data, after)


class Gather:
    def __init__(self, near, hubs, table, sem, bs):
        below, below_edge, own, above, above_edge = near
        plain = own.shape[0]
        size = plain * bs
        z = lax.axis_index("var") % SIDE

        def copy(ref, at):
            return pltpu.make_async_copy(ref.reshape(size, ref.shape[2]), table.at[pl.ds(at, size), :], sem)

        self.choices = [
            (z == 0, copy(below, 0), copy(below_edge, 0)),
            (z == SIDE - 1, copy(above, 2 * size), copy(above_edge, 2 * size)),
        ]
        self.copies = [copy(own, size)]
        at = 3 * size
        for ref in hubs:
            for i in range(ref.shape[0]):
                self.copies.append(
                    pltpu.make_async_copy(
                        ref.at[i, pl.ds(0, HUB_DEV * bs), :],
                        table.at[pl.ds(at, HUB_DEV * bs), :],
                        sem,
                    )
                )
                at += HUB_DEV * bs

    def start(self):
        for copy in self.copies:
            copy.start()
        for edge, usual, other in self.choices:
            pl.when(edge)(other.start)
            pl.when(jnp.logical_not(edge))(usual.start)

    def wait(self):
        for copy in self.copies:
            copy.wait()
        for _, usual, _ in self.choices:
            usual.wait()


def fill_lookup(pattern, ids, order, inverse, lookup):
    rows, slots = pattern.shape
    plain = rows - HUB_DEV
    base = lax.axis_index("var") * rows

    def clear(i, _):
        inverse[base + i] = -1
        return 0

    lax.fori_loop(0, 3 * rows, clear, 0)

    def mark(q, _):
        inverse[ids[q] + rows] = 3 * plain + q
        return 0

    lax.fori_loop(0, ids.shape[0], mark, 0)
    for side in range(3):

        def place(i, found):
            at = base + side * rows + i
            seen = inverse[at]
            inverse[at] = jnp.where(seen < 0, side * plain + found, seen)
            return found + jnp.where(seen < 0, 1, 0)

        lax.fori_loop(0, rows, place, jnp.int32(0))
    total = 3 * plain + ids.shape[0]
    for p in range(rows):
        for k in range(slots if p < HUB_DEV else HALF):
            c = inverse[pattern[order[p], k] + rows]
            lookup[slot_base(p, slots) + k] = jnp.clip(c, 0, total - 1)


def image_group(tile_of, blocks_of, live, bs):
    high, low, blocks = [], [], []
    for k in range(GROUP):
        tile = tile_of(k)
        if live is not None:
            tile = jnp.where(k < live, tile, 0.0)
        top = tile.astype(BF)
        high.append(top)
        low.append((tile - top.astype(F32)).astype(BF))
        blocks.append(blocks_of(k))
    left = jnp.concatenate([jnp.concatenate(high, axis=1), jnp.concatenate(low, axis=1)], axis=0)
    both = jnp.dot(left, jnp.concatenate(blocks, axis=0), preferred_element_type=F32)
    return both[:bs] + both[bs:]


def hub_images(tile_of, lookup, table, out, slots, bs):
    for p in range(HUB_DEV):
        total = None
        for start in range(p * slots, (p + 1) * slots, GROUP):
            part = image_group(
                lambda k: tile_of(start + k),
                lambda k: table[aligned(lookup[start + k], bs), :],
                None,
                bs,
            )
            total = part if total is None else total + part
        out[p * bs : (p + 1) * bs, :] = total.astype(BF)


def plain_images(counts, order, ready, tile_of, lookup, table, out, slots, bs):
    def one(p, _):
        ready(p)
        start = HUB_DEV * slots + p * HALF
        image = image_group(
            lambda k: tile_of(p * HALF + k),
            lambda k: table[aligned(lookup[start + k], bs), :],
            counts[order[HUB_DEV + p]],
            bs,
        )
        out[p] = image.astype(BF)
        return 0

    lax.fori_loop(0, out.shape[0], one, 0, unroll=2)


def first_hub_kernel(*refs):
    counts, pattern, ids, omega = refs[:4]
    near, hubs = refs[4:9], refs[9:13]
    out, lookup, table, rows_out = refs[13:17]
    order, inverse, tiles, table_sem, tile_sem = refs[17:]
    rows, slots = pattern.shape
    bs, share = tiles.shape[1], rows_out.shape[1]
    row_order(counts, order, slots)
    gather = Gather(near, hubs, table, table_sem, bs)
    gather.start()
    part = aligned(lax.axis_index("samp"), share)
    moves = []
    for p in range(rows):
        n = slots if p < HUB_DEV else HALF
        at = pl.ds(slot_base(p, slots), n)
        moves.append(
            pltpu.make_async_copy(omega.at[order[p], pl.ds(0, n), part], rows_out.at[at], tile_sem)
        )
        if p < HUB_DEV:
            moves.append(pltpu.make_async_copy(omega.at[order[p]], tiles.at[at], tile_sem))
    for move in moves:
        move.start()
    fill_lookup(pattern, ids, order, inverse, lookup)
    for move in moves:
        move.wait()
    gather.wait()
    hub_images(lambda s: tiles[s], lookup, table, out, slots, bs)


def first_hub(counts, pattern, ids, omega, near, hubs, part_count):
    rows, slots, bs, _ = omega.shape
    total = HUB_DEV * slots + (rows - HUB_DEV) * HALF
    local = hubs[0].shape[2]
    table = (3 * (rows - HUB_DEV) + SIDE * SIDE * HUB_DEV) * bs
    return pl.pallas_call(
        first_hub_kernel,
        out_shape=(
            jax.ShapeDtypeStruct((HUB_DEV * bs, local), BF),
            jax.ShapeDtypeStruct((total,), jnp.int32),
            jax.ShapeDtypeStruct((table, local), BF),
            jax.ShapeDtypeStruct((total, bs // part_count, bs), F32),
        ),
        in_specs=[SMEM, SMEM, SMEM] + [ANY] * 10,
        out_specs=(VMEM, SMEM, VMEM, VMEM),
        scratch_shapes=[
            pltpu.SMEM((rows,), jnp.int32),
            pltpu.SMEM((rows * (SIDE * SIDE + 2),), jnp.int32),
            pltpu.VMEM((HUB_DEV * slots, bs, bs), F32),
            pltpu.SemaphoreType.DMA,
            pltpu.SemaphoreType.DMA,
        ],
        compiler_params=grant(16),
        cost_estimate=cost(1 << 28, 12 << 20),
        name="hub_first",
    )(counts, pattern, ids, omega, *near, *hubs)


def first_plain_kernel(slots, *refs):
    counts, lookup, omega, table, _, out = refs[:6]
    order, tiles, sems = refs[6:]
    bs = tiles.shape[1]
    row_order(counts, order, slots)

    def move(p):
        return pltpu.make_async_copy(
            omega.at[order[HUB_DEV + p], pl.ds(0, HALF)], tiles.at[pl.ds(p * HALF, HALF)], sems.at[p]
        )

    for p in range(out.shape[0]):
        move(p).start()
    plain_images(
        counts, order, lambda p: move(p).wait(), lambda s: tiles[s], lookup, table, out, slots, bs
    )


def first_plain(counts, lookup, omega, table, after):
    rows, slots, bs, _ = omega.shape
    plain = rows - HUB_DEV
    return pl.pallas_call(
        lambda *refs: first_plain_kernel(slots, *refs),
        out_shape=jax.ShapeDtypeStruct((plain, bs, table.shape[1]), BF),
        in_specs=[SMEM, SMEM, ANY, VMEM, ANY],
        out_specs=VMEM,
        scratch_shapes=[
            pltpu.SMEM((rows,), jnp.int32),
            pltpu.VMEM((plain * HALF, bs, bs), F32),
            pltpu.SemaphoreType.DMA((plain,)),
        ],
        compiler_params=grant(16),
        cost_estimate=cost(1 << 29, 10 << 20),
        name="plain_first",
    )(counts, lookup, omega, table, after)


def wire_scales(tail, scales):
    exponent = tail.astype(jnp.int32).astype(F32).reshape(scales.shape)
    scales[...] = jnp.exp2(exponent) * (1.0 / LEVELS)


def to_wire(read, out, scales, total):
    scales[...] = jnp.ones_like(scales)

    def peak(s, _):
        scales[pl.ds(s, 1), :] = jnp.max(jnp.abs(read(s)), axis=0, keepdims=True)
        return 0

    lax.fori_loop(0, total, peak, 0, unroll=8)
    exponent = jnp.ceil(jnp.log2(jnp.maximum(scales[...], TINY)))
    tail = exponent.reshape(-1, *out.shape[1:])
    out[total:] = tail.astype(jnp.int32).astype(WIRE)
    scales[...] = jnp.exp2(-exponent) * LEVELS

    def put(s, _):
        out[s] = jnp.round(read(s) * scales[pl.ds(s, 1), :]).astype(jnp.int32).astype(WIRE)
        return 0

    lax.fori_loop(0, total, put, 0, unroll=8)


def wire_shape(total, share, bs):
    return (total + -(-total // share), share, bs)


def later_kernel(slots, hub, *refs):
    counts, lookup, mine, partner, table, _, out = refs[:7]
    order, levels, tails, scales, sem = refs[7:]
    total, bs = lookup.shape[0], levels.shape[1]
    share = mine.shape[2]
    first = 0 if hub else HUB_DEV * slots
    row_order(counts, order, slots)
    part = lax.axis_index("samp")
    moves = []
    for j in range(SIDE):
        for ref, core in ((mine, part % CORES), (partner, (part + 1) % CORES)):
            at = ((part // CORES + j) % SIDE) * CORES + core
            moves.append(
                pltpu.make_async_copy(
                    ref.at[j, pl.ds(first, levels.shape[0])],
                    levels.at[:, aligned(at, share), :],
                    sem,
                )
            )
            moves.append(
                pltpu.make_async_copy(
                    ref.at[j, pl.ds(total, mine.shape[1] - total)], tails.at[at], sem
                )
            )
    for move in moves:
        move.start()
    for move in moves:
        move.wait()
    for g in range(SIDE * CORES):
        wire_scales(tails[g], scales.at[g])

    def tile_of(s):
        rows = [
            levels[s, g * share : (g + 1) * share, :].astype(jnp.int32).astype(F32)
            * scales[g, pl.ds(first + s, 1), :]
            for g in range(SIDE * CORES)
        ]
        return jnp.concatenate(rows, axis=0)

    if hub:
        hub_images(tile_of, lookup, table, out, slots, bs)
    else:
        plain_images(
            counts, order, lambda p: None, tile_of, lookup, table, out, slots, bs
        )


def later_image(counts, lookup, mine, partner, table, slots, after):
    total = lookup.shape[0]
    plain = counts.shape[0] - HUB_DEV
    _, long, share, bs = mine.shape
    local = table.shape[1]
    groups = SIDE * CORES
    hub = after is None
    count = HUB_DEV * slots if hub else plain * HALF
    return pl.pallas_call(
        lambda *refs: later_kernel(slots, hub, *refs),
        out_shape=jax.ShapeDtypeStruct(
            (HUB_DEV * bs, local) if hub else (plain, bs, local), BF
        ),
        in_specs=[SMEM, SMEM, ANY, ANY, VMEM, ANY],
        out_specs=VMEM,
        scratch_shapes=[
            pltpu.SMEM(counts.shape, jnp.int32),
            pltpu.VMEM((count, bs, bs), WIRE),
            pltpu.VMEM((groups, long - total, share, bs), WIRE),
            pltpu.VMEM((groups, (long - total) * share, bs), F32),
            pltpu.SemaphoreType.DMA,
        ],
        compiler_params=grant(16),
        cost_estimate=cost(1 << 28 if hub else 1 << 29, (2 if hub else 8) << 20),
        name="hub_later" if hub else "plain_later",
    )(counts, lookup, mine, partner, table, counts if hub else after)


def gradient_kernel(scale, slots, *refs):
    lookup, x_table = refs[:2]
    near, hubs = refs[2:7], refs[7:11]
    keep, send, m_table, sem = refs[11:]
    plain, bs, _ = near[0].shape
    gather = Gather(near, hubs, m_table, sem, bs)
    gather.start()
    gather.wait()
    part = lax.axis_index("samp")
    y, core = part // CORES, part % CORES
    share = keep.shape[2]

    def group(start, own):
        mine = aligned(own, bs)
        left = jnp.concatenate([m_table[mine, :], x_table[mine, :]], axis=1)
        right = []
        for k in range(GROUP):
            at = aligned(lookup[start + k], bs)
            right.append(jnp.concatenate([x_table[at, :], m_table[at, :]], axis=1))
        both = lax.dot_general(
            left,
            jnp.concatenate(right, axis=0),
            (((1,), (1,)), ((), ())),
            preferred_element_type=F32,
        )
        both = both * scale
        for k in range(GROUP):
            tile = both[:, k * bs : (k + 1) * bs].reshape(SIDE, CORES, share, bs)
            even, odd = tile[:, 0], tile[:, 1]
            stay = jnp.where(core == 0, even, odd)
            leave = jnp.where(core == 0, odd, even)
            for g in range(SIDE):
                to = (g + SIDE - y) % SIDE
                keep[to, start + k] = stay[g]
                send[to, start + k] = leave[g]

    for p in range(HUB_DEV):
        for start in range(p * slots, (p + 1) * slots, GROUP):
            group(start, 3 * plain + p)

    def step(p, _):
        group(HUB_DEV * slots + p * HALF, plain + p)
        return 0

    lax.fori_loop(0, plain, step, 0, unroll=2)


def gradient(lookup, table, near, hubs, scale, slots, part_count):
    total = lookup.shape[0]
    bs = near[0].shape[1]
    shape = jax.ShapeDtypeStruct((SIDE, total, bs // part_count, bs), F32)
    return pl.pallas_call(
        lambda *refs: gradient_kernel(scale, slots, *refs),
        out_shape=(shape, shape),
        in_specs=[SMEM, VMEM] + [ANY] * 9,
        out_specs=(VMEM, VMEM),
        scratch_shapes=[pltpu.VMEM(table.shape, BF), pltpu.SemaphoreType.DMA],
        compiler_params=grant(24),
        cost_estimate=cost(1 << 30, 16 << 20),
        name="gradient",
    )(lookup, table, *near, *hubs)


def add_kernel(keep, other, own, *refs):
    sends, total_sum, scales = refs[:-2], refs[-2], refs[-1]
    total = own.shape[0]
    own[...] = keep[0] + other[0]
    for j, ref in enumerate(sends):
        total_sum[...] = keep[j + 1] + other[j + 1]
        to_wire(lambda s: total_sum[s], ref, scales, total)


def add_cores(keep, other):
    side, total, share, bs = keep.shape
    wire = jax.ShapeDtypeStruct(wire_shape(total, share, bs), WIRE)
    return pl.pallas_call(
        add_kernel,
        out_shape=(jax.ShapeDtypeStruct((total, share, bs), F32),) + (wire,) * (side - 1),
        in_specs=[VMEM, VMEM],
        out_specs=(VMEM,) * side,
        scratch_shapes=[
            pltpu.VMEM((total, share, bs), F32),
            pltpu.VMEM(((wire.shape[0] - total) * share, bs), F32),
        ],
        compiler_params=grant(16),
        name="add_cores",
    )(keep, other)


def new_tile(tile, slope, leading, live, part, share):
    stepped = tile - STEP_SIZE * slope
    edge = STEP_SIZE * PENALTY
    shrunk = stepped - jnp.minimum(jnp.maximum(stepped, -edge), edge)
    if leading:
        shape = stepped.shape
        row = part * share + lax.broadcasted_iota(jnp.int32, shape, 0)
        col = lax.broadcasted_iota(jnp.int32, shape, 1)
        barrier = 0.5 * (stepped + jnp.sqrt(stepped * stepped + 4.0 * STEP_SIZE))
        shrunk = jnp.where(row == col, barrier, shrunk)
    return jnp.where(live, shrunk, 0.0)


def prox_kernel(last, slots, counts, tiles, own, *refs):
    sends = refs[: SIDE - 1]
    outs = refs[SIDE - 1 : -2]
    order, scales = refs[-2:]
    rows = order.shape[0]
    row_order(counts, order, slots)
    part = lax.axis_index("samp")
    total, share, bs = own.shape
    for j, ref in enumerate(sends):
        wire_scales(ref[total:], scales.at[j])

    def slot(row, s, k, n):
        slope = own[s]
        for j, ref in enumerate(sends):
            slope = slope + ref[s].astype(jnp.int32).astype(F32) * scales[j, pl.ds(s, 1), :]
        value = new_tile(tiles[s], slope, k == 0, k < n, part, share)
        if last:
            outs[0][row, k] = value
        else:
            outs[0][s] = value

    for p in range(HUB_DEV):
        for k in range(slots):
            slot(order[p], p * slots + k, k, slots)

    def plain(p, _):
        row = order[HUB_DEV + p]
        n = counts[row]
        for k in range(HALF):
            slot(row, HUB_DEV * slots + p * HALF + k, k, n)
        if last:
            for k in range(HALF, slots):
                outs[0][row, k] = jnp.zeros((share, bs), F32)
        return 0

    lax.fori_loop(0, rows - HUB_DEV, plain, 0, unroll=2)
    if not last:
        to_wire(lambda s: outs[0][s], outs[1], scales.at[0], total)


def prox(counts, tiles, terms, slots, last):
    rows = counts.shape[0]
    total, share, bs = tiles.shape
    wire = wire_shape(total, share, bs)
    if last:
        outs = (jax.ShapeDtypeStruct((rows, slots, share, bs), F32),)
    else:
        outs = (jax.ShapeDtypeStruct((total, share, bs), F32), jax.ShapeDtypeStruct(wire, WIRE))
    return pl.pallas_call(
        lambda *refs: prox_kernel(last, slots, *refs),
        out_shape=outs,
        in_specs=[SMEM] + [VMEM] * 5,
        out_specs=(VMEM,) * len(outs),
        scratch_shapes=[
            pltpu.SMEM((rows,), jnp.int32),
            pltpu.VMEM((SIDE - 1, (wire[0] - total) * share, bs), F32),
        ],
        compiler_params=grant(16),
        name="prox_last" if last else "prox",
    )(counts, tiles, *terms)


def share_near(value):
    size = lax.axis_size("var")
    up = [(i, i + 1) for i in range(size - 1)]
    moves = []
    for pairs in (up, [(j, i) for i, j in up]):
        inner = [(i, j) for i, j in pairs if i // SIDE == j // SIDE]
        edge = [(i, j) for i, j in pairs if i // SIDE != j // SIDE]
        crossing = lax.ppermute(value, "var", edge)
        moves.append((crossing, lax.ppermute(value, "var", inner)))
    (below_edge, below), (above_edge, above) = moves
    return below, below_edge, value, above, above_edge


def share_hubs(value):
    by_z = [value] + [lax.ppermute(value, "var", var_shift(0, d)) for d in (1, -1, 2)]
    column = jnp.stack(by_z)
    return [column] + [lax.ppermute(column, "var", var_shift(d, 0)) for d in (1, -1, 2)]


def per_device(data, omega, pattern, counts):
    parts = lax.axis_size("samp")
    _, slots, bs, _ = omega.shape
    scale = 0.5 / (data.shape[0] * parts)
    x_hub = pack_hub(data, counts, slots, bs)
    x_hubs = share_hubs(x_hub)
    x_own = pack_plain(data, counts, slots, bs, x_hub)
    x_near = share_near(x_own)
    ids = jnp.stack([g[:, HUB_DEV * bs : HUB_DEV * bs + HUB_DEV, 0] for g in x_hubs])
    ids = ids.reshape(-1).astype(jnp.int32)
    for iteration in range(ITERS):
        if iteration == 0:
            m_hub, lookup, table, tiles = first_hub(
                counts, pattern, ids, omega, x_near, x_hubs, parts
            )
        else:
            mine = jnp.stack(
                [
                    sent,
                    lax.ppermute(sent, "samp", samp_shift(-1, 0)),
                    lax.ppermute(sent, "samp", samp_shift(2, 0)),
                    lax.ppermute(sent, "samp", samp_shift(1, 0)),
                ]
            )
            partner = lax.ppermute(mine, "samp", samp_shift(0, 1))
            m_hub = later_image(counts, lookup, mine, partner, table, slots, None)
        m_hubs = share_hubs(m_hub)
        if iteration == 0:
            m_own = first_plain(counts, lookup, omega, table, m_hub)
        else:
            m_own = later_image(counts, lookup, mine, partner, table, slots, m_hub)
        m_near = share_near(m_own)
        keep, leave = gradient(lookup, table, m_near, m_hubs, scale, slots, parts)
        other = lax.ppermute(leave, "samp", samp_shift(0, 1))
        own, up, across, down = add_cores(keep, other)
        terms = (
            own,
            lax.ppermute(up, "samp", samp_shift(1, 0)),
            lax.ppermute(across, "samp", samp_shift(2, 0)),
            lax.ppermute(down, "samp", samp_shift(-1, 0)),
        )
        if iteration < ITERS - 1:
            tiles, sent = prox(counts, tiles, terms, slots, False)
        else:
            (tiles,) = prox(counts, tiles, terms, slots, True)
    return tiles


def solution(mesh):
    placed = (P("samp", "var"), P("var", None, None, None), P("var", None), P("var"))
    return jax.shard_map(
        per_device,
        mesh=mesh,
        in_specs=placed,
        out_specs=P("var", None, "samp", None),
        check_vma=False,
    )
```

```python
import jax
import jax.numpy as jnp
from jax import lax
from jax.experimental import pallas as pl
from jax.experimental.pallas import tpu as pltpu
from jax.sharding import PartitionSpec as P


HUB_DEV = 2
ITERS = 2
STEP_SIZE = 0.25
PENALTY = 1.0
HALF = 4
GROUP = 4
SIDE = 4
CORES = 2
LEVELS = 32000.0
TINY = 1e-30
BF = jnp.bfloat16
F32 = jnp.float32
WIRE = jnp.int16
ANY = pl.BlockSpec(memory_space=pl.ANY)
SMEM = pl.BlockSpec(memory_space=pltpu.SMEM)
VMEM = pl.BlockSpec(memory_space=pltpu.VMEM)


def grant(mib):
    return pltpu.CompilerParams(vmem_limit_bytes=mib << 20)


def cost(flops, moved):
    return pl.CostEstimate(flops=flops, bytes_accessed=moved, transcendentals=0)


def var_shift(dx, dz):
    return [
        (x * SIDE + z, ((x + dx) % SIDE) * SIDE + (z + dz) % SIDE)
        for x in range(SIDE)
        for z in range(SIDE)
    ]


def samp_shift(dy, dc):
    return [
        (y * CORES + c, ((y + dy) % SIDE) * CORES + (c + dc) % CORES)
        for y in range(SIDE)
        for c in range(CORES)
    ]


def row_order(counts, order, slots):
    def step(r, carry):
        hubs, others = carry
        hub = jnp.where(counts[r] == slots, 1, 0)
        order[jnp.where(hub == 1, hubs, HUB_DEV + others)] = r
        return hubs + hub, others + 1 - hub

    lax.fori_loop(0, order.shape[0], step, (jnp.int32(0), jnp.int32(0)))


def slot_base(p, slots):
    return p * slots if p < HUB_DEV else HUB_DEV * slots + (p - HUB_DEV) * HALF


def aligned(index, size):
    return pl.ds(pl.multiple_of(index * size, size), size)


def turned(data, row, bs):
    shape = (bs, bs)
    eye = lax.broadcasted_iota(jnp.int32, shape, 0) == lax.broadcasted_iota(jnp.int32, shape, 1)
    block = data[:, aligned(row, bs)]
    return lax.dot_general(
        eye.astype(F32).astype(BF), block, (((1,), (1,)), ((), ())), preferred_element_type=F32
    ).astype(BF)


def pack_hub_kernel(slots, bs, counts, data, out, order):
    row_order(counts, order, slots)
    first = lax.axis_index("var") * order.shape[0]
    for p in range(HUB_DEV):
        out[p * bs : (p + 1) * bs, :] = turned(data, order[p], bs)
    tail = out.shape[0] - HUB_DEV * bs
    lead = lax.broadcasted_iota(jnp.int32, (tail, out.shape[1]), 0) == 0
    ids = jnp.where(lead, first + order[0], first + order[1])
    out[HUB_DEV * bs :, :] = ids.astype(F32).astype(BF)


def pack_plain_kernel(slots, bs, counts, data, _, out, order):
    row_order(counts, order, slots)
    for p in range(out.shape[0]):
        out[p] = turned(data, order[HUB_DEV + p], bs)


def pack_hub(data, counts, slots, bs):
    return pl.pallas_call(
        lambda *refs: pack_hub_kernel(slots, bs, *refs),
        out_shape=jax.ShapeDtypeStruct((HUB_DEV * bs + 16, data.shape[0]), BF),
        in_specs=[SMEM, VMEM],
        out_specs=VMEM,
        scratch_shapes=[pltpu.SMEM(counts.shape, jnp.int32)],
        compiler_params=grant(8),
        cost_estimate=cost(1 << 20, 1 << 20),
        name="pack_hub",
    )(counts, data)


def pack_plain(data, counts, slots, bs, after):
    return pl.pallas_call(
        lambda *refs: pack_plain_kernel(slots, bs, *refs),
        out_shape=jax.ShapeDtypeStruct((counts.shape[0] - HUB_DEV, bs, data.shape[0]), BF),
        in_specs=[SMEM, VMEM, ANY],
        out_specs=VMEM,
        scratch_shapes=[pltpu.SMEM(counts.shape, jnp.int32)],
        compiler_params=grant(8),
        cost_estimate=cost(1 << 20, 1 << 20),
        name="pack_plain",
    )(counts, data, after)


class Gather:
    def __init__(self, near, hubs, table, sem, bs):
        below, own, above, crossing, turn = near
        size = own.shape[0] * bs
        z = lax.axis_index("var") % SIDE

        def copy(ref, at):
            rows = ref.shape[0] * bs
            return pltpu.make_async_copy(
                ref.reshape(rows, ref.shape[2]), table.at[pl.ds(at, rows), :], sem
            )

        self.choices = []
        for edge, usual, at in ((z == 0, below, 0), (z == SIDE - 1, above, 2 * size)):
            pair = [copy(crossing, at), copy(turn, at + crossing.shape[0] * bs)]
            self.choices.append((edge, copy(usual, at), pair))
        self.copies = [copy(own, size)]
        at = 3 * size
        for ref in hubs:
            for i in range(ref.shape[0]):
                self.copies.append(
                    pltpu.make_async_copy(
                        ref.at[i, pl.ds(0, HUB_DEV * bs), :],
                        table.at[pl.ds(at, HUB_DEV * bs), :],
                        sem,
                    )
                )
                at += HUB_DEV * bs

    def start(self):
        for copy in self.copies:
            copy.start()
        for edge, usual, pair in self.choices:
            for other in pair:
                pl.when(edge)(other.start)
            pl.when(jnp.logical_not(edge))(usual.start)

    def wait(self):
        for copy in self.copies:
            copy.wait()
        for _, usual, _ in self.choices:
            usual.wait()


def fill_lookup(pattern, ids, order, inverse, lookup):
    rows, slots = pattern.shape
    plain = rows - HUB_DEV
    base = lax.axis_index("var") * rows

    def clear(i, _):
        inverse[base + i] = -1
        return 0

    lax.fori_loop(0, 3 * rows, clear, 0)

    def mark(q, _):
        inverse[ids[q] + rows] = 3 * plain + q
        return 0

    lax.fori_loop(0, ids.shape[0], mark, 0)
    for side in range(3):

        def place(i, found):
            at = base + side * rows + i
            seen = inverse[at]
            inverse[at] = jnp.where(seen < 0, side * plain + found, seen)
            return found + jnp.where(seen < 0, 1, 0)

        lax.fori_loop(0, rows, place, jnp.int32(0))
    total = 3 * plain + ids.shape[0]
    for p in range(rows):
        for k in range(slots if p < HUB_DEV else HALF):
            c = inverse[pattern[order[p], k] + rows]
            lookup[slot_base(p, slots) + k] = jnp.clip(c, 0, total - 1)


def image_group(tile_of, blocks_of, live, bs):
    high, low, blocks = [], [], []
    for k in range(GROUP):
        tile = tile_of(k)
        if live is not None:
            tile = jnp.where(k < live, tile, 0.0)
        top = tile.astype(BF)
        high.append(top)
        low.append((tile - top.astype(F32)).astype(BF))
        blocks.append(blocks_of(k))
    left = jnp.concatenate([jnp.concatenate(high, axis=1), jnp.concatenate(low, axis=1)], axis=0)
    both = jnp.dot(left, jnp.concatenate(blocks, axis=0), preferred_element_type=F32)
    return both[:bs] + both[bs:]


def hub_images(tile_of, lookup, table, out, slots, bs):
    for p in range(HUB_DEV):
        total = None
        for start in range(p * slots, (p + 1) * slots, GROUP):
            part = image_group(
                lambda k: tile_of(start + k),
                lambda k: table[aligned(lookup[start + k], bs), :],
                None,
                bs,
            )
            total = part if total is None else total + part
        out[p * bs : (p + 1) * bs, :] = total.astype(BF)


def plain_images(counts, order, ready, tile_of, lookup, table, out, slots, bs):
    def one(p, _):
        ready(p)
        start = HUB_DEV * slots + p * HALF
        image = image_group(
            lambda k: tile_of(p * HALF + k),
            lambda k: table[aligned(lookup[start + k], bs), :],
            counts[order[HUB_DEV + p]],
            bs,
        )
        out[p] = image.astype(BF)
        return 0

    lax.fori_loop(0, out.shape[0], one, 0, unroll=2)


def first_hub_kernel(*refs):
    counts, pattern, ids, omega = refs[:4]
    near, hubs = refs[4:9], refs[9:14]
    out, lookup, table, rows_out = refs[14:18]
    order, inverse, tiles, table_sem, tile_sem = refs[18:]
    rows, slots = pattern.shape
    bs, share = tiles.shape[1], rows_out.shape[1]
    row_order(counts, order, slots)
    gather = Gather(near, hubs, table, table_sem, bs)
    gather.start()
    part = aligned(lax.axis_index("samp"), share)
    moves = []
    for p in range(rows):
        n = slots if p < HUB_DEV else HALF
        at = pl.ds(slot_base(p, slots), n)
        moves.append(
            pltpu.make_async_copy(omega.at[order[p], pl.ds(0, n), part], rows_out.at[at], tile_sem)
        )
        if p < HUB_DEV:
            moves.append(pltpu.make_async_copy(omega.at[order[p]], tiles.at[at], tile_sem))
    for move in moves:
        move.start()
    fill_lookup(pattern, ids, order, inverse, lookup)
    for move in moves:
        move.wait()
    gather.wait()
    hub_images(lambda s: tiles[s], lookup, table, out, slots, bs)


def first_hub(counts, pattern, ids, omega, near, hubs, part_count):
    rows, slots, bs, _ = omega.shape
    total = HUB_DEV * slots + (rows - HUB_DEV) * HALF
    local = hubs[0].shape[2]
    table = (3 * (rows - HUB_DEV) + SIDE * SIDE * HUB_DEV) * bs
    return pl.pallas_call(
        first_hub_kernel,
        out_shape=(
            jax.ShapeDtypeStruct((HUB_DEV * bs, local), BF),
            jax.ShapeDtypeStruct((total,), jnp.int32),
            jax.ShapeDtypeStruct((table, local), BF),
            jax.ShapeDtypeStruct((total, bs // part_count, bs), F32),
        ),
        in_specs=[SMEM, SMEM, SMEM] + [ANY] * 11,
        out_specs=(VMEM, SMEM, VMEM, VMEM),
        scratch_shapes=[
            pltpu.SMEM((rows,), jnp.int32),
            pltpu.SMEM((rows * (SIDE * SIDE + 2),), jnp.int32),
            pltpu.VMEM((HUB_DEV * slots, bs, bs), F32),
            pltpu.SemaphoreType.DMA,
            pltpu.SemaphoreType.DMA,
        ],
        compiler_params=grant(16),
        cost_estimate=cost(1 << 28, 12 << 20),
        name="hub_first",
    )(counts, pattern, ids, omega, *near, *hubs)


def first_plain_kernel(slots, *refs):
    counts, lookup, omega, table, _, out = refs[:6]
    order, tiles, sems = refs[6:]
    bs = tiles.shape[1]
    row_order(counts, order, slots)

    def move(p):
        return pltpu.make_async_copy(
            omega.at[order[HUB_DEV + p], pl.ds(0, HALF)], tiles.at[pl.ds(p * HALF, HALF)], sems.at[p]
        )

    for p in range(out.shape[0]):
        move(p).start()
    plain_images(
        counts, order, lambda p: move(p).wait(), lambda s: tiles[s], lookup, table, out, slots, bs
    )


def first_plain(counts, lookup, omega, table, after):
    rows, slots, bs, _ = omega.shape
    plain = rows - HUB_DEV
    return pl.pallas_call(
        lambda *refs: first_plain_kernel(slots, *refs),
        out_shape=jax.ShapeDtypeStruct((plain, bs, table.shape[1]), BF),
        in_specs=[SMEM, SMEM, ANY, VMEM, ANY],
        out_specs=VMEM,
        scratch_shapes=[
            pltpu.SMEM((rows,), jnp.int32),
            pltpu.VMEM((plain * HALF, bs, bs), F32),
            pltpu.SemaphoreType.DMA((plain,)),
        ],
        compiler_params=grant(16),
        cost_estimate=cost(1 << 29, 10 << 20),
        name="plain_first",
    )(counts, lookup, omega, table, after)


def wire_scales(tail, scales):
    exponent = tail.astype(jnp.int32).astype(F32).reshape(scales.shape)
    scales[...] = jnp.exp2(exponent) * (1.0 / LEVELS)


def to_wire(read, out, scales, total):
    scales[...] = jnp.ones_like(scales)

    def peak(s, _):
        scales[pl.ds(s, 1), :] = jnp.max(jnp.abs(read(s)), axis=0, keepdims=True)
        return 0

    lax.fori_loop(0, total, peak, 0, unroll=8)
    exponent = jnp.ceil(jnp.log2(jnp.maximum(scales[...], TINY)))
    tail = exponent.reshape(-1, *out.shape[1:])
    out[total:] = tail.astype(jnp.int32).astype(WIRE)
    scales[...] = jnp.exp2(-exponent) * LEVELS

    def put(s, _):
        out[s] = jnp.round(read(s) * scales[pl.ds(s, 1), :]).astype(jnp.int32).astype(WIRE)
        return 0

    lax.fori_loop(0, total, put, 0, unroll=8)


def wire_shape(total, share, bs):
    return (total + -(-total // share), share, bs)


def later_kernel(slots, hub, *refs):
    counts, lookup, mine, partner, table, _, out = refs[:7]
    order, levels, tails, scales, sem = refs[7:]
    total, bs = lookup.shape[0], levels.shape[1]
    share = mine.shape[2]
    first = 0 if hub else HUB_DEV * slots
    row_order(counts, order, slots)
    part = lax.axis_index("samp")
    moves = []
    for j in range(SIDE):
        for ref, core in ((mine, part % CORES), (partner, (part + 1) % CORES)):
            at = ((part // CORES + j) % SIDE) * CORES + core
            moves.append(
                pltpu.make_async_copy(
                    ref.at[j, pl.ds(first, levels.shape[0])],
                    levels.at[:, aligned(at, share), :],
                    sem,
                )
            )
            moves.append(
                pltpu.make_async_copy(
                    ref.at[j, pl.ds(total, mine.shape[1] - total)], tails.at[at], sem
                )
            )
    for move in moves:
        move.start()
    for move in moves:
        move.wait()
    for g in range(SIDE * CORES):
        wire_scales(tails[g], scales.at[g])

    def tile_of(s):
        rows = [
            levels[s, g * share : (g + 1) * share, :].astype(jnp.int32).astype(F32)
            * scales[g, pl.ds(first + s, 1), :]
            for g in range(SIDE * CORES)
        ]
        return jnp.concatenate(rows, axis=0)

    if hub:
        hub_images(tile_of, lookup, table, out, slots, bs)
    else:
        plain_images(
            counts, order, lambda p: None, tile_of, lookup, table, out, slots, bs
        )


def later_image(counts, lookup, mine, partner, table, slots, after):
    total = lookup.shape[0]
    plain = counts.shape[0] - HUB_DEV
    _, long, share, bs = mine.shape
    local = table.shape[1]
    groups = SIDE * CORES
    hub = after is None
    count = HUB_DEV * slots if hub else plain * HALF
    return pl.pallas_call(
        lambda *refs: later_kernel(slots, hub, *refs),
        out_shape=jax.ShapeDtypeStruct(
            (HUB_DEV * bs, local) if hub else (plain, bs, local), BF
        ),
        in_specs=[SMEM, SMEM, ANY, ANY, VMEM, ANY],
        out_specs=VMEM,
        scratch_shapes=[
            pltpu.SMEM(counts.shape, jnp.int32),
            pltpu.VMEM((count, bs, bs), WIRE),
            pltpu.VMEM((groups, long - total, share, bs), WIRE),
            pltpu.VMEM((groups, (long - total) * share, bs), F32),
            pltpu.SemaphoreType.DMA,
        ],
        compiler_params=grant(16),
        cost_estimate=cost(1 << 28 if hub else 1 << 29, (2 if hub else 8) << 20),
        name="hub_later" if hub else "plain_later",
    )(counts, lookup, mine, partner, table, counts if hub else after)


def gradient_kernel(scale, slots, *refs):
    lookup, x_table = refs[:2]
    near, hubs = refs[2:7], refs[7:12]
    keep, send, m_table, sem = refs[12:]
    plain, bs, _ = near[1].shape
    gather = Gather(near, hubs, m_table, sem, bs)
    gather.start()
    gather.wait()
    part = lax.axis_index("samp")
    y, core = part // CORES, part % CORES
    share = keep.shape[2]

    def group(start, own):
        mine = aligned(own, bs)
        left = jnp.concatenate([m_table[mine, :], x_table[mine, :]], axis=1)
        right = []
        for k in range(GROUP):
            at = aligned(lookup[start + k], bs)
            right.append(jnp.concatenate([x_table[at, :], m_table[at, :]], axis=1))
        both = lax.dot_general(
            left,
            jnp.concatenate(right, axis=0),
            (((1,), (1,)), ((), ())),
            preferred_element_type=F32,
        )
        both = both * scale
        for k in range(GROUP):
            tile = both[:, k * bs : (k + 1) * bs].reshape(SIDE, CORES, share, bs)
            even, odd = tile[:, 0], tile[:, 1]
            stay = jnp.where(core == 0, even, odd)
            leave = jnp.where(core == 0, odd, even)
            for g in range(SIDE):
                to = (g + SIDE - y) % SIDE
                keep[to, start + k] = stay[g]
                send[to, start + k] = leave[g]

    for p in range(HUB_DEV):
        for start in range(p * slots, (p + 1) * slots, GROUP):
            group(start, 3 * plain + p)

    def step(p, _):
        group(HUB_DEV * slots + p * HALF, plain + p)
        return 0

    lax.fori_loop(0, plain, step, 0, unroll=2)


def gradient(lookup, table, near, hubs, scale, slots, part_count):
    total = lookup.shape[0]
    bs = near[0].shape[1]
    shape = jax.ShapeDtypeStruct((SIDE, total, bs // part_count, bs), F32)
    return pl.pallas_call(
        lambda *refs: gradient_kernel(scale, slots, *refs),
        out_shape=(shape, shape),
        in_specs=[SMEM, VMEM] + [ANY] * 10,
        out_specs=(VMEM, VMEM),
        scratch_shapes=[pltpu.VMEM(table.shape, BF), pltpu.SemaphoreType.DMA],
        compiler_params=grant(24),
        cost_estimate=cost(1 << 30, 16 << 20),
        name="gradient",
    )(lookup, table, *near, *hubs)


def add_kernel(keep, other, own, *refs):
    sends, total_sum, scales = refs[:-2], refs[-2], refs[-1]
    total = own.shape[0]
    own[...] = keep[0] + other[0]
    for j, ref in enumerate(sends):
        total_sum[...] = keep[j + 1] + other[j + 1]
        to_wire(lambda s: total_sum[s], ref, scales, total)


def add_cores(keep, other):
    side, total, share, bs = keep.shape
    wire = jax.ShapeDtypeStruct(wire_shape(total, share, bs), WIRE)
    return pl.pallas_call(
        add_kernel,
        out_shape=(jax.ShapeDtypeStruct((total, share, bs), F32),) + (wire,) * (side - 1),
        in_specs=[VMEM, VMEM],
        out_specs=(VMEM,) * side,
        scratch_shapes=[
            pltpu.VMEM((total, share, bs), F32),
            pltpu.VMEM(((wire.shape[0] - total) * share, bs), F32),
        ],
        compiler_params=grant(16),
        name="add_cores",
    )(keep, other)


def new_tile(tile, slope, leading, live, part, share):
    stepped = tile - STEP_SIZE * slope
    edge = STEP_SIZE * PENALTY
    shrunk = stepped - jnp.minimum(jnp.maximum(stepped, -edge), edge)
    if leading:
        shape = stepped.shape
        row = part * share + lax.broadcasted_iota(jnp.int32, shape, 0)
        col = lax.broadcasted_iota(jnp.int32, shape, 1)
        barrier = 0.5 * (stepped + jnp.sqrt(stepped * stepped + 4.0 * STEP_SIZE))
        shrunk = jnp.where(row == col, barrier, shrunk)
    return jnp.where(live, shrunk, 0.0)


def prox_kernel(last, slots, counts, tiles, own, *refs):
    sends = refs[: SIDE - 1]
    outs = refs[SIDE - 1 : -2]
    order, scales = refs[-2:]
    rows = order.shape[0]
    row_order(counts, order, slots)
    part = lax.axis_index("samp")
    total, share, bs = own.shape
    for j, ref in enumerate(sends):
        wire_scales(ref[total:], scales.at[j])

    def slot(row, s, k, n):
        slope = own[s]
        for j, ref in enumerate(sends):
            slope = slope + ref[s].astype(jnp.int32).astype(F32) * scales[j, pl.ds(s, 1), :]
        value = new_tile(tiles[s], slope, k == 0, k < n, part, share)
        if last:
            outs[0][row, k] = value
        else:
            outs[0][s] = value

    for p in range(HUB_DEV):
        for k in range(slots):
            slot(order[p], p * slots + k, k, slots)

    def plain(p, _):
        row = order[HUB_DEV + p]
        n = counts[row]
        for k in range(HALF):
            slot(row, HUB_DEV * slots + p * HALF + k, k, n)
        if last:
            for k in range(HALF, slots):
                outs[0][row, k] = jnp.zeros((share, bs), F32)
        return 0

    lax.fori_loop(0, rows - HUB_DEV, plain, 0, unroll=2)
    if not last:
        to_wire(lambda s: outs[0][s], outs[1], scales.at[0], total)


def prox(counts, tiles, terms, slots, last):
    rows = counts.shape[0]
    total, share, bs = tiles.shape
    wire = wire_shape(total, share, bs)
    if last:
        outs = (jax.ShapeDtypeStruct((rows, slots, share, bs), F32),)
    else:
        outs = (jax.ShapeDtypeStruct((total, share, bs), F32), jax.ShapeDtypeStruct(wire, WIRE))
    return pl.pallas_call(
        lambda *refs: prox_kernel(last, slots, *refs),
        out_shape=outs,
        in_specs=[SMEM] + [VMEM] * 5,
        out_specs=(VMEM,) * len(outs),
        scratch_shapes=[
            pltpu.SMEM((rows,), jnp.int32),
            pltpu.VMEM((SIDE - 1, (wire[0] - total) * share, bs), F32),
        ],
        compiler_params=grant(16),
        name="prox_last" if last else "prox",
    )(counts, tiles, *terms)


def share_near(value):
    last = lax.axis_size("var") // SIDE - 1
    size = lax.axis_size("var")
    far = SIDE - 1
    direct, there, over = [], [], []
    for x in range(last):
        low, high = x * SIDE, (x + 1) * SIDE
        direct += [(low + far, high), (high, low + far)]
        there += [(low + far, low), (high, high + far)]
        over += [(low, high), (high + far, low + far)]
    half = value.shape[0] // 2
    crossing = lax.ppermute(value[:half], "var", direct)
    turn = lax.ppermute(value[half:], "var", there)
    turn = lax.ppermute(turn, "var", over)
    up = [(i, i + 1) for i in range(size - 1) if (i + 1) % SIDE]
    below = lax.ppermute(value, "var", up)
    above = lax.ppermute(value, "var", [(j, i) for i, j in up])
    return below, value, above, crossing, turn


def share_hubs(value):
    by_z = [value] + [lax.ppermute(value, "var", var_shift(0, d)) for d in (1, -1, 2)]
    column = jnp.stack(by_z)
    half = SIDE // 2
    ahead = lax.ppermute(column, "var", var_shift(1, 0))
    behind = lax.ppermute(column, "var", var_shift(-1, 0))
    across = [
        lax.ppermute(ahead[:half], "var", var_shift(1, 0)),
        lax.ppermute(behind[half:], "var", var_shift(-1, 0)),
    ]
    return [column, ahead, behind] + across


def per_device(data, omega, pattern, counts):
    parts = lax.axis_size("samp")
    _, slots, bs, _ = omega.shape
    scale = 0.5 / (data.shape[0] * parts)
    x_hub = pack_hub(data, counts, slots, bs)
    x_hubs = share_hubs(x_hub)
    x_own = pack_plain(data, counts, slots, bs, x_hub)
    x_near = share_near(x_own)
    ids = jnp.concatenate([g[:, HUB_DEV * bs : HUB_DEV * bs + HUB_DEV, 0] for g in x_hubs])
    ids = ids.reshape(-1).astype(jnp.int32)
    for iteration in range(ITERS):
        if iteration == 0:
            m_hub, lookup, table, tiles = first_hub(
                counts, pattern, ids, omega, x_near, x_hubs, parts
            )
        else:
            mine = jnp.stack(
                [
                    sent,
                    lax.ppermute(sent, "samp", samp_shift(-1, 0)),
                    lax.ppermute(sent, "samp", samp_shift(2, 0)),
                    lax.ppermute(sent, "samp", samp_shift(1, 0)),
                ]
            )
            partner = lax.ppermute(mine, "samp", samp_shift(0, 1))
            m_hub = later_image(counts, lookup, mine, partner, table, slots, None)
        m_hubs = share_hubs(m_hub)
        if iteration == 0:
            m_own = first_plain(counts, lookup, omega, table, m_hub)
        else:
            m_own = later_image(counts, lookup, mine, partner, table, slots, m_hub)
        m_near = share_near(m_own)
        keep, leave = gradient(lookup, table, m_near, m_hubs, scale, slots, parts)
        other = lax.ppermute(leave, "samp", samp_shift(0, 1))
        own, up, across, down = add_cores(keep, other)
        terms = (
            own,
            lax.ppermute(up, "samp", samp_shift(1, 0)),
            lax.ppermute(across, "samp", samp_shift(2, 0)),
            lax.ppermute(down, "samp", samp_shift(-1, 0)),
        )
        if iteration < ITERS - 1:
            tiles, sent = prox(counts, tiles, terms, slots, False)
        else:
            (tiles,) = prox(counts, tiles, terms, slots, True)
    return tiles


def solution(mesh):
    placed = (P("samp", "var"), P("var", None, None, None), P("var", None), P("var"))
    return jax.shard_map(
        per_device,
        mesh=mesh,
        in_specs=placed,
        out_specs=P("var", None, "samp", None),
        check_vma=False,
    )
```

```python
import jax
import jax.numpy as jnp
from jax import lax
from jax.experimental import pallas as pl
from jax.experimental.pallas import tpu as pltpu
from jax.sharding import PartitionSpec as P


HUB_DEV = 2
ITERS = 2
STEP_SIZE = 0.25
PENALTY = 1.0
HALF = 4
GROUP = 4
SIDE = 4
CORES = 2
LEVELS = 32000.0
TINY = 1e-30
BF = jnp.bfloat16
F32 = jnp.float32
WIRE = jnp.int16
ANY = pl.BlockSpec(memory_space=pl.ANY)
SMEM = pl.BlockSpec(memory_space=pltpu.SMEM)
VMEM = pl.BlockSpec(memory_space=pltpu.VMEM)


def grant(mib):
    return pltpu.CompilerParams(vmem_limit_bytes=mib << 20)


def cost(flops, moved):
    return pl.CostEstimate(flops=flops, bytes_accessed=moved, transcendentals=0)


def var_shift(dx, dz):
    return [
        (x * SIDE + z, ((x + dx) % SIDE) * SIDE + (z + dz) % SIDE)
        for x in range(SIDE)
        for z in range(SIDE)
    ]


def samp_shift(dy, dc):
    return [
        (y * CORES + c, ((y + dy) % SIDE) * CORES + (c + dc) % CORES)
        for y in range(SIDE)
        for c in range(CORES)
    ]


def row_order(counts, order, slots):
    def step(r, carry):
        hubs, others = carry
        hub = jnp.where(counts[r] == slots, 1, 0)
        order[jnp.where(hub == 1, hubs, HUB_DEV + others)] = r
        return hubs + hub, others + 1 - hub

    lax.fori_loop(0, order.shape[0], step, (jnp.int32(0), jnp.int32(0)))


def slot_base(p, slots):
    return p * slots if p < HUB_DEV else HUB_DEV * slots + (p - HUB_DEV) * HALF


def aligned(index, size):
    return pl.ds(pl.multiple_of(index * size, size), size)


def turned(data, row, bs):
    shape = (bs, bs)
    eye = lax.broadcasted_iota(jnp.int32, shape, 0) == lax.broadcasted_iota(jnp.int32, shape, 1)
    block = data[:, aligned(row, bs)]
    return lax.dot_general(
        eye.astype(F32).astype(BF), block, (((1,), (1,)), ((), ())), preferred_element_type=F32
    ).astype(BF)


def pack_hub_kernel(slots, bs, counts, data, out, order):
    row_order(counts, order, slots)
    first = lax.axis_index("var") * order.shape[0]
    for p in range(HUB_DEV):
        out[p * bs : (p + 1) * bs, :] = turned(data, order[p], bs)
    tail = out.shape[0] - HUB_DEV * bs
    lead = lax.broadcasted_iota(jnp.int32, (tail, out.shape[1]), 0) == 0
    ids = jnp.where(lead, first + order[0], first + order[1])
    out[HUB_DEV * bs :, :] = ids.astype(F32).astype(BF)


def pack_plain_kernel(slots, bs, counts, data, _, out, order):
    row_order(counts, order, slots)
    for p in range(out.shape[0]):
        out[p] = turned(data, order[HUB_DEV + p], bs)


def pack_hub(data, counts, slots, bs):
    return pl.pallas_call(
        lambda *refs: pack_hub_kernel(slots, bs, *refs),
        out_shape=jax.ShapeDtypeStruct((HUB_DEV * bs + 16, data.shape[0]), BF),
        in_specs=[SMEM, VMEM],
        out_specs=VMEM,
        scratch_shapes=[pltpu.SMEM(counts.shape, jnp.int32)],
        compiler_params=grant(8),
        cost_estimate=cost(1 << 20, 1 << 20),
        name="pack_hub",
    )(counts, data)


def pack_plain(data, counts, slots, bs, after):
    return pl.pallas_call(
        lambda *refs: pack_plain_kernel(slots, bs, *refs),
        out_shape=jax.ShapeDtypeStruct((counts.shape[0] - HUB_DEV, bs, data.shape[0]), BF),
        in_specs=[SMEM, VMEM, ANY],
        out_specs=VMEM,
        scratch_shapes=[pltpu.SMEM(counts.shape, jnp.int32)],
        compiler_params=grant(8),
        cost_estimate=cost(1 << 20, 1 << 20),
        name="pack_plain",
    )(counts, data, after)


class Gather:
    def __init__(self, near, hubs, table, sem, bs):
        below, own, above, crossing, turn = near
        size = own.shape[0] * bs
        z = lax.axis_index("var") % SIDE

        def copy(ref, at):
            rows = ref.shape[0] * bs
            return pltpu.make_async_copy(
                ref.reshape(rows, ref.shape[2]), table.at[pl.ds(at, rows), :], sem
            )

        self.choices = []
        for edge, usual, at in ((z == 0, below, 0), (z == SIDE - 1, above, 2 * size)):
            pair = [copy(crossing, at), copy(turn, at + crossing.shape[0] * bs)]
            self.choices.append((edge, copy(usual, at), pair))
        self.copies = [copy(own, size)]
        at = 3 * size
        for ref in hubs:
            for i in range(ref.shape[0]):
                self.copies.append(
                    pltpu.make_async_copy(
                        ref.at[i, pl.ds(0, HUB_DEV * bs), :],
                        table.at[pl.ds(at, HUB_DEV * bs), :],
                        sem,
                    )
                )
                at += HUB_DEV * bs

    def start(self):
        for copy in self.copies:
            copy.start()
        for edge, usual, pair in self.choices:
            for other in pair:
                pl.when(edge)(other.start)
            pl.when(jnp.logical_not(edge))(usual.start)

    def wait(self):
        for copy in self.copies:
            copy.wait()
        for _, usual, _ in self.choices:
            usual.wait()


def fill_lookup(pattern, ids, order, inverse, lookup):
    rows, slots = pattern.shape
    plain = rows - HUB_DEV
    base = lax.axis_index("var") * rows

    def clear(i, _):
        inverse[base + i] = -1
        return 0

    lax.fori_loop(0, 3 * rows, clear, 0)

    def mark(q, _):
        inverse[ids[q] + rows] = 3 * plain + q
        return 0

    lax.fori_loop(0, ids.shape[0], mark, 0)
    for side in range(3):

        def place(i, found):
            at = base + side * rows + i
            seen = inverse[at]
            inverse[at] = jnp.where(seen < 0, side * plain + found, seen)
            return found + jnp.where(seen < 0, 1, 0)

        lax.fori_loop(0, rows, place, jnp.int32(0))
    total = 3 * plain + ids.shape[0]
    for p in range(rows):
        for k in range(slots if p < HUB_DEV else HALF):
            c = inverse[pattern[order[p], k] + rows]
            lookup[slot_base(p, slots) + k] = jnp.clip(c, 0, total - 1)


def halves(tile_of, live):
    high, low = [], []
    for k in range(GROUP):
        tile = tile_of(k)
        if live is not None:
            tile = jnp.where(k < live, tile, 0.0)
        top = tile.astype(BF)
        high.append(top)
        low.append((tile - top.astype(F32)).astype(BF))
    return jnp.concatenate([jnp.concatenate(high, axis=1), jnp.concatenate(low, axis=1)], axis=0)


def image_group(left, lookup, table, start, bs):
    blocks = [table[aligned(lookup[start + k], bs), :] for k in range(GROUP)]
    both = jnp.dot(left, jnp.concatenate(blocks, axis=0), preferred_element_type=F32)
    return both[:bs] + both[bs:]


def hub_images(left_of, lookup, table, out, slots, bs):
    for p in range(HUB_DEV):
        total = None
        for start in range(p * slots, (p + 1) * slots, GROUP):
            part = image_group(left_of(start // GROUP), lookup, table, start, bs)
            total = part if total is None else total + part
        out[p * bs : (p + 1) * bs, :] = total.astype(BF)


def plain_images(left_of, lookup, table, out, slots, bs):
    first = HUB_DEV * slots

    def one(p, _):
        left = left_of(p)
        out[p] = image_group(left, lookup, table, first + p * HALF, bs).astype(BF)
        return 0

    lax.fori_loop(0, out.shape[0], one, 0, unroll=2)


def prep_kernel(counts, omega, left_hub, left, rows_out, order, tiles, part_sem, sems):
    rows, slots, _, _ = omega.shape
    share = rows_out.shape[1]
    row_order(counts, order, slots)
    part = aligned(lax.axis_index("samp"), share)
    whole, parts = [], []
    for p in range(rows):
        n = slots if p < HUB_DEV else HALF
        at = pl.ds(slot_base(p, slots), n)
        whole.append(
            pltpu.make_async_copy(omega.at[order[p], pl.ds(0, n)], tiles.at[at], sems.at[p])
        )
        parts.append(
            pltpu.make_async_copy(omega.at[order[p], pl.ds(0, n), part], rows_out.at[at], part_sem)
        )
    for move in whole + parts:
        move.start()
    for p in range(rows):
        whole[p].wait()
        start = slot_base(p, slots)
        live = None if p < HUB_DEV else counts[order[p]]
        for s in range(start, start + (slots if p < HUB_DEV else HALF), GROUP):
            g = s // GROUP
            if p < HUB_DEV:
                left_hub[g] = halves(lambda k: tiles[s + k], live)
            else:
                left[g - left_hub.shape[0]] = halves(lambda k: tiles[s + k], live)
    for move in parts:
        move.wait()


def prep(counts, omega, part_count):
    rows, slots, bs, _ = omega.shape
    total = HUB_DEV * slots + (rows - HUB_DEV) * HALF
    return pl.pallas_call(
        prep_kernel,
        out_shape=(
            jax.ShapeDtypeStruct((HUB_DEV * slots // GROUP, 2 * bs, GROUP * bs), BF),
            jax.ShapeDtypeStruct((rows - HUB_DEV, 2 * bs, GROUP * bs), BF),
            jax.ShapeDtypeStruct((total, bs // part_count, bs), F32),
        ),
        in_specs=[SMEM, ANY],
        out_specs=(VMEM, VMEM, VMEM),
        scratch_shapes=[
            pltpu.SMEM((rows,), jnp.int32),
            pltpu.VMEM((total, bs, bs), F32),
            pltpu.SemaphoreType.DMA,
            pltpu.SemaphoreType.DMA((rows,)),
        ],
        compiler_params=grant(48),
        cost_estimate=cost(1 << 24, 12 << 20),
        name="prep",
    )(counts, omega)


def first_hub_kernel(*refs):
    counts, pattern, ids, left = refs[:4]
    near, hubs = refs[4:9], refs[9:14]
    out, lookup, table = refs[14:17]
    order, inverse, sem = refs[17:]
    slots = pattern.shape[1]
    bs = left.shape[1] // 2
    row_order(counts, order, slots)
    gather = Gather(near, hubs, table, sem, bs)
    gather.start()
    fill_lookup(pattern, ids, order, inverse, lookup)
    gather.wait()
    hub_images(lambda g: left[g], lookup, table, out, slots, bs)


def first_hub(counts, pattern, ids, left, near, hubs):
    rows, slots = pattern.shape
    total = HUB_DEV * slots + (rows - HUB_DEV) * HALF
    bs = left.shape[1] // 2
    local = hubs[0].shape[2]
    table = (3 * (rows - HUB_DEV) + SIDE * SIDE * HUB_DEV) * bs
    return pl.pallas_call(
        first_hub_kernel,
        out_shape=(
            jax.ShapeDtypeStruct((HUB_DEV * bs, local), BF),
            jax.ShapeDtypeStruct((total,), jnp.int32),
            jax.ShapeDtypeStruct((table, local), BF),
        ),
        in_specs=[SMEM, SMEM, SMEM, VMEM] + [ANY] * 10,
        out_specs=(VMEM, SMEM, VMEM),
        scratch_shapes=[
            pltpu.SMEM((rows,), jnp.int32),
            pltpu.SMEM((rows * (SIDE * SIDE + 2),), jnp.int32),
            pltpu.SemaphoreType.DMA,
        ],
        compiler_params=grant(12),
        cost_estimate=cost(1 << 28, 12 << 20),
        name="hub_first",
    )(counts, pattern, ids, left, *near, *hubs)


def first_plain_kernel(slots, lookup, left, table, _, out):
    bs = out.shape[1]
    plain_images(lambda p: left[p], lookup, table, out, slots, bs)


def first_plain(lookup, left, table, slots, after):
    bs = left.shape[1] // 2
    plain = (lookup.shape[0] - HUB_DEV * slots) // HALF
    return pl.pallas_call(
        lambda *refs: first_plain_kernel(slots, *refs),
        out_shape=jax.ShapeDtypeStruct((plain, bs, table.shape[1]), BF),
        in_specs=[SMEM, VMEM, VMEM, ANY],
        out_specs=VMEM,
        compiler_params=grant(12),
        cost_estimate=cost(1 << 29, 10 << 20),
        name="plain_first",
    )(lookup, left, table, after)


def wire_scales(tail, scales):
    exponent = tail.astype(jnp.int32).astype(F32).reshape(scales.shape)
    scales[...] = jnp.exp2(exponent) * (1.0 / LEVELS)


def to_wire(read, out, scales, total):
    scales[...] = jnp.ones_like(scales)

    def peak(s, _):
        scales[pl.ds(s, 1), :] = jnp.max(jnp.abs(read(s)), axis=0, keepdims=True)
        return 0

    lax.fori_loop(0, total, peak, 0, unroll=8)
    exponent = jnp.ceil(jnp.log2(jnp.maximum(scales[...], TINY)))
    tail = exponent.reshape(-1, *out.shape[1:])
    out[total:] = tail.astype(jnp.int32).astype(WIRE)
    scales[...] = jnp.exp2(-exponent) * LEVELS

    def put(s, _):
        out[s] = jnp.round(read(s) * scales[pl.ds(s, 1), :]).astype(jnp.int32).astype(WIRE)
        return 0

    lax.fori_loop(0, total, put, 0, unroll=8)


def wire_shape(total, share, bs):
    return (total + -(-total // share), share, bs)


def later_kernel(slots, hub, *refs):
    counts, lookup, mine, partner, table, _, out = refs[:7]
    order, levels, tails, scales, sem = refs[7:]
    total, bs = lookup.shape[0], levels.shape[1]
    share = mine.shape[2]
    first = 0 if hub else HUB_DEV * slots
    row_order(counts, order, slots)
    part = lax.axis_index("samp")
    moves = []
    for j in range(SIDE):
        for ref, core in ((mine, part % CORES), (partner, (part + 1) % CORES)):
            at = ((part // CORES + j) % SIDE) * CORES + core
            moves.append(
                pltpu.make_async_copy(
                    ref.at[j, pl.ds(first, levels.shape[0])],
                    levels.at[:, aligned(at, share), :],
                    sem,
                )
            )
            moves.append(
                pltpu.make_async_copy(
                    ref.at[j, pl.ds(total, mine.shape[1] - total)], tails.at[at], sem
                )
            )
    for move in moves:
        move.start()
    for move in moves:
        move.wait()
    for g in range(SIDE * CORES):
        wire_scales(tails[g], scales.at[g])

    def tile_of(s):
        rows = [
            levels[s, g * share : (g + 1) * share, :].astype(jnp.int32).astype(F32)
            * scales[g, pl.ds(first + s, 1), :]
            for g in range(SIDE * CORES)
        ]
        return jnp.concatenate(rows, axis=0)

    if hub:
        hub_images(
            lambda g: halves(lambda k: tile_of(g * GROUP + k), None), lookup, table, out, slots, bs
        )
    else:
        plain_images(
            lambda p: halves(lambda k: tile_of(p * HALF + k), counts[order[HUB_DEV + p]]),
            lookup,
            table,
            out,
            slots,
            bs,
        )


def later_image(counts, lookup, mine, partner, table, slots, after):
    total = lookup.shape[0]
    plain = counts.shape[0] - HUB_DEV
    _, long, share, bs = mine.shape
    local = table.shape[1]
    groups = SIDE * CORES
    hub = after is None
    count = HUB_DEV * slots if hub else plain * HALF
    return pl.pallas_call(
        lambda *refs: later_kernel(slots, hub, *refs),
        out_shape=jax.ShapeDtypeStruct(
            (HUB_DEV * bs, local) if hub else (plain, bs, local), BF
        ),
        in_specs=[SMEM, SMEM, ANY, ANY, VMEM, ANY],
        out_specs=VMEM,
        scratch_shapes=[
            pltpu.SMEM(counts.shape, jnp.int32),
            pltpu.VMEM((count, bs, bs), WIRE),
            pltpu.VMEM((groups, long - total, share, bs), WIRE),
            pltpu.VMEM((groups, (long - total) * share, bs), F32),
            pltpu.SemaphoreType.DMA,
        ],
        compiler_params=grant(16),
        cost_estimate=cost(1 << 28 if hub else 1 << 29, (2 if hub else 8) << 20),
        name="hub_later" if hub else "plain_later",
    )(counts, lookup, mine, partner, table, counts if hub else after)


def groups(slots, plain, term):
    for p in range(HUB_DEV):
        for start in range(p * slots, (p + 1) * slots, GROUP):
            term(start, 3 * plain + p)

    def step(p, _):
        term(HUB_DEV * slots + p * HALF, plain + p)
        return 0

    lax.fori_loop(0, plain, step, 0, unroll=2)


def product(own, lookup, table, start, bs):
    right = [table[aligned(lookup[start + k], bs), :] for k in range(GROUP)]
    return lax.dot_general(
        own, jnp.concatenate(right, axis=0), (((1,), (1,)), ((), ())), preferred_element_type=F32
    )


def firsts_kernel(slots, lookup, x_table, m_own, m_hub, out):
    plain, bs, _ = m_own.shape
    for p in range(HUB_DEV):
        for start in range(p * slots, (p + 1) * slots, GROUP):
            own = m_hub[p * bs : (p + 1) * bs, :]
            out[start // GROUP] = product(own, lookup, x_table, start, bs)

    def step(p, _):
        start = HUB_DEV * slots + p * HALF
        out[HUB_DEV * slots // GROUP + p] = product(m_own[p], lookup, x_table, start, bs)
        return 0

    lax.fori_loop(0, plain, step, 0, unroll=2)


def first_terms(lookup, table, m_own, m_hub, slots):
    bs = m_own.shape[1]
    return pl.pallas_call(
        lambda *refs: firsts_kernel(slots, *refs),
        out_shape=jax.ShapeDtypeStruct((lookup.shape[0] // GROUP, bs, GROUP * bs), F32),
        in_specs=[SMEM, VMEM, VMEM, VMEM],
        out_specs=VMEM,
        compiler_params=grant(12),
        cost_estimate=cost(1 << 29, 10 << 20),
        name="firsts",
    )(lookup, table, m_own, m_hub)


def gradient_kernel(scale, slots, *refs):
    lookup, x_table, firsts = refs[:3]
    near, hubs = refs[3:8], refs[8:13]
    keep, send, m_table, sem = refs[13:]
    plain, bs, _ = near[1].shape
    gather = Gather(near, hubs, m_table, sem, bs)
    gather.start()
    gather.wait()
    part = lax.axis_index("samp")
    y, core = part // CORES, part % CORES
    share = keep.shape[2]

    def group(start, own):
        term = product(x_table[aligned(own, bs), :], lookup, m_table, start, bs)
        both = (firsts[start // GROUP] + term) * scale
        for k in range(GROUP):
            tile = both[:, k * bs : (k + 1) * bs].reshape(SIDE, CORES, share, bs)
            even, odd = tile[:, 0], tile[:, 1]
            stay = jnp.where(core == 0, even, odd)
            leave = jnp.where(core == 0, odd, even)
            for g in range(SIDE):
                to = (g + SIDE - y) % SIDE
                keep[to, start + k] = stay[g]
                send[to, start + k] = leave[g]

    groups(slots, plain, group)


def gradient(lookup, table, firsts, near, hubs, scale, slots, part_count):
    total = lookup.shape[0]
    bs = firsts.shape[1]
    shape = jax.ShapeDtypeStruct((SIDE, total, bs // part_count, bs), F32)
    return pl.pallas_call(
        lambda *refs: gradient_kernel(scale, slots, *refs),
        out_shape=(shape, shape),
        in_specs=[SMEM, VMEM, VMEM] + [ANY] * 10,
        out_specs=(VMEM, VMEM),
        scratch_shapes=[pltpu.VMEM(table.shape, BF), pltpu.SemaphoreType.DMA],
        compiler_params=grant(20),
        cost_estimate=cost(1 << 30, 16 << 20),
        name="gradient",
    )(lookup, table, firsts, *near, *hubs)


def add_kernel(keep, other, own, *refs):
    sends, total_sum, scales = refs[:-2], refs[-2], refs[-1]
    total = own.shape[0]
    own[...] = keep[0] + other[0]
    for j, ref in enumerate(sends):
        total_sum[...] = keep[j + 1] + other[j + 1]
        to_wire(lambda s: total_sum[s], ref, scales, total)


def add_cores(keep, other):
    side, total, share, bs = keep.shape
    wire = jax.ShapeDtypeStruct(wire_shape(total, share, bs), WIRE)
    return pl.pallas_call(
        add_kernel,
        out_shape=(jax.ShapeDtypeStruct((total, share, bs), F32),) + (wire,) * (side - 1),
        in_specs=[VMEM, VMEM],
        out_specs=(VMEM,) * side,
        scratch_shapes=[
            pltpu.VMEM((total, share, bs), F32),
            pltpu.VMEM(((wire.shape[0] - total) * share, bs), F32),
        ],
        compiler_params=grant(16),
        name="add_cores",
    )(keep, other)


def new_tile(tile, slope, leading, live, part, share):
    stepped = tile - STEP_SIZE * slope
    edge = STEP_SIZE * PENALTY
    shrunk = stepped - jnp.minimum(jnp.maximum(stepped, -edge), edge)
    if leading:
        shape = stepped.shape
        row = part * share + lax.broadcasted_iota(jnp.int32, shape, 0)
        col = lax.broadcasted_iota(jnp.int32, shape, 1)
        barrier = 0.5 * (stepped + jnp.sqrt(stepped * stepped + 4.0 * STEP_SIZE))
        shrunk = jnp.where(row == col, barrier, shrunk)
    return jnp.where(live, shrunk, 0.0)


def prox_kernel(last, slots, counts, tiles, own, *refs):
    sends = refs[: SIDE - 1]
    outs = refs[SIDE - 1 : -2]
    order, scales = refs[-2:]
    rows = order.shape[0]
    row_order(counts, order, slots)
    part = lax.axis_index("samp")
    total, share, bs = own.shape
    for j, ref in enumerate(sends):
        wire_scales(ref[total:], scales.at[j])

    def slot(row, s, k, n):
        slope = own[s]
        for j, ref in enumerate(sends):
            slope = slope + ref[s].astype(jnp.int32).astype(F32) * scales[j, pl.ds(s, 1), :]
        value = new_tile(tiles[s], slope, k == 0, k < n, part, share)
        if last:
            outs[0][row, k] = value
        else:
            outs[0][s] = value

    for p in range(HUB_DEV):
        for k in range(slots):
            slot(order[p], p * slots + k, k, slots)

    def plain(p, _):
        row = order[HUB_DEV + p]
        n = counts[row]
        for k in range(HALF):
            slot(row, HUB_DEV * slots + p * HALF + k, k, n)
        if last:
            for k in range(HALF, slots):
                outs[0][row, k] = jnp.zeros((share, bs), F32)
        return 0

    lax.fori_loop(0, rows - HUB_DEV, plain, 0, unroll=2)
    if not last:
        to_wire(lambda s: outs[0][s], outs[1], scales.at[0], total)


def prox(counts, tiles, terms, slots, last):
    rows = counts.shape[0]
    total, share, bs = tiles.shape
    wire = wire_shape(total, share, bs)
    if last:
        outs = (jax.ShapeDtypeStruct((rows, slots, share, bs), F32),)
    else:
        outs = (jax.ShapeDtypeStruct((total, share, bs), F32), jax.ShapeDtypeStruct(wire, WIRE))
    return pl.pallas_call(
        lambda *refs: prox_kernel(last, slots, *refs),
        out_shape=outs,
        in_specs=[SMEM] + [VMEM] * 5,
        out_specs=(VMEM,) * len(outs),
        scratch_shapes=[
            pltpu.SMEM((rows,), jnp.int32),
            pltpu.VMEM((SIDE - 1, (wire[0] - total) * share, bs), F32),
        ],
        compiler_params=grant(16),
        name="prox_last" if last else "prox",
    )(counts, tiles, *terms)


def share_near(value):
    last = lax.axis_size("var") // SIDE - 1
    size = lax.axis_size("var")
    far = SIDE - 1
    direct, there, over = [], [], []
    for x in range(last):
        low, high = x * SIDE, (x + 1) * SIDE
        direct += [(low + far, high), (high, low + far)]
        there += [(low + far, low), (high, high + far)]
        over += [(low, high), (high + far, low + far)]
    half = value.shape[0] // 2
    crossing = lax.ppermute(value[:half], "var", direct)
    turn = lax.ppermute(value[half:], "var", there)
    turn = lax.ppermute(turn, "var", over)
    up = [(i, i + 1) for i in range(size - 1) if (i + 1) % SIDE]
    below = lax.ppermute(value, "var", up)
    above = lax.ppermute(value, "var", [(j, i) for i, j in up])
    return below, value, above, crossing, turn


def share_hubs(value):
    by_z = [value] + [lax.ppermute(value, "var", var_shift(0, d)) for d in (1, -1, 2)]
    column = jnp.stack(by_z)
    half = SIDE // 2
    ahead = lax.ppermute(column, "var", var_shift(1, 0))
    behind = lax.ppermute(column, "var", var_shift(-1, 0))
    across = [
        lax.ppermute(ahead[:half], "var", var_shift(1, 0)),
        lax.ppermute(behind[half:], "var", var_shift(-1, 0)),
    ]
    return [column, ahead, behind] + across


def per_device(data, omega, pattern, counts):
    parts = lax.axis_size("samp")
    _, slots, bs, _ = omega.shape
    scale = 0.5 / (data.shape[0] * parts)
    x_hub = pack_hub(data, counts, slots, bs)
    x_hubs = share_hubs(x_hub)
    x_own = pack_plain(data, counts, slots, bs, x_hub)
    x_near = share_near(x_own)
    left_hub, left, tiles = prep(counts, omega, parts)
    ids = jnp.concatenate([g[:, HUB_DEV * bs : HUB_DEV * bs + HUB_DEV, 0] for g in x_hubs])
    ids = ids.reshape(-1).astype(jnp.int32)
    for iteration in range(ITERS):
        if iteration == 0:
            m_hub, lookup, table = first_hub(counts, pattern, ids, left_hub, x_near, x_hubs)
        else:
            mine = jnp.stack(
                [
                    sent,
                    lax.ppermute(sent, "samp", samp_shift(-1, 0)),
                    lax.ppermute(sent, "samp", samp_shift(2, 0)),
                    lax.ppermute(sent, "samp", samp_shift(1, 0)),
                ]
            )
            partner = lax.ppermute(mine, "samp", samp_shift(0, 1))
            m_hub = later_image(counts, lookup, mine, partner, table, slots, None)
        m_hubs = share_hubs(m_hub)
        if iteration == 0:
            m_own = first_plain(lookup, left, table, slots, m_hub)
        else:
            m_own = later_image(counts, lookup, mine, partner, table, slots, m_hub)
        m_near = share_near(m_own)
        firsts = first_terms(lookup, table, m_own, m_hub, slots)
        keep, leave = gradient(lookup, table, firsts, m_near, m_hubs, scale, slots, parts)
        other = lax.ppermute(leave, "samp", samp_shift(0, 1))
        own, up, across, down = add_cores(keep, other)
        terms = (
            own,
            lax.ppermute(up, "samp", samp_shift(1, 0)),
            lax.ppermute(across, "samp", samp_shift(2, 0)),
            lax.ppermute(down, "samp", samp_shift(-1, 0)),
        )
        if iteration < ITERS - 1:
            tiles, sent = prox(counts, tiles, terms, slots, False)
        else:
            (tiles,) = prox(counts, tiles, terms, slots, True)
    return tiles


def solution(mesh):
    placed = (P("samp", "var"), P("var", None, None, None), P("var", None), P("var"))
    return jax.shard_map(
        per_device,
        mesh=mesh,
        in_specs=placed,
        out_specs=P("var", None, "samp", None),
        check_vma=False,
    )
```

```python
import jax
import jax.numpy as jnp
from jax import lax
from jax.experimental import pallas as pl
from jax.experimental.pallas import tpu as pltpu
from jax.sharding import PartitionSpec as P


HUB_DEV = 2
ITERS = 2
STEP_SIZE = 0.25
PENALTY = 1.0
HALF = 4
GROUP = 4
SIDE = 4
CORES = 2
LEVELS = 32000.0
TINY = 1e-30
BF = jnp.bfloat16
F32 = jnp.float32
WIRE = jnp.int16
ANY = pl.BlockSpec(memory_space=pl.ANY)
SMEM = pl.BlockSpec(memory_space=pltpu.SMEM)
VMEM = pl.BlockSpec(memory_space=pltpu.VMEM)


def grant(mib):
    return pltpu.CompilerParams(vmem_limit_bytes=mib << 20)


def cost(flops, moved):
    return pl.CostEstimate(flops=flops, bytes_accessed=moved, transcendentals=0)


def var_shift(dx, dz):
    return [
        (x * SIDE + z, ((x + dx) % SIDE) * SIDE + (z + dz) % SIDE)
        for x in range(SIDE)
        for z in range(SIDE)
    ]


def samp_shift(dy, dc):
    return [
        (y * CORES + c, ((y + dy) % SIDE) * CORES + (c + dc) % CORES)
        for y in range(SIDE)
        for c in range(CORES)
    ]


def row_order(counts, order, slots):
    def step(r, carry):
        hubs, others = carry
        hub = jnp.where(counts[r] == slots, 1, 0)
        order[jnp.where(hub == 1, hubs, HUB_DEV + others)] = r
        return hubs + hub, others + 1 - hub

    lax.fori_loop(0, order.shape[0], step, (jnp.int32(0), jnp.int32(0)))


def slot_base(p, slots):
    return p * slots if p < HUB_DEV else HUB_DEV * slots + (p - HUB_DEV) * HALF


def aligned(index, size):
    return pl.ds(pl.multiple_of(index * size, size), size)


def turned(data, row, bs):
    shape = (bs, bs)
    eye = lax.broadcasted_iota(jnp.int32, shape, 0) == lax.broadcasted_iota(jnp.int32, shape, 1)
    block = data[:, aligned(row, bs)]
    return lax.dot_general(
        eye.astype(F32).astype(BF), block, (((1,), (1,)), ((), ())), preferred_element_type=F32
    ).astype(BF)


def pack_hub_kernel(slots, bs, counts, data, out, order):
    row_order(counts, order, slots)
    first = lax.axis_index("var") * order.shape[0]
    for p in range(HUB_DEV):
        out[p * bs : (p + 1) * bs, :] = turned(data, order[p], bs)
    tail = out.shape[0] - HUB_DEV * bs
    lead = lax.broadcasted_iota(jnp.int32, (tail, out.shape[1]), 0) == 0
    ids = jnp.where(lead, first + order[0], first + order[1])
    out[HUB_DEV * bs :, :] = ids.astype(F32).astype(BF)


def pack_plain_kernel(slots, bs, counts, data, _, out, order):
    row_order(counts, order, slots)
    for p in range(out.shape[0]):
        out[p] = turned(data, order[HUB_DEV + p], bs)


def pack_hub(data, counts, slots, bs):
    return pl.pallas_call(
        lambda *refs: pack_hub_kernel(slots, bs, *refs),
        out_shape=jax.ShapeDtypeStruct((HUB_DEV * bs + 16, data.shape[0]), BF),
        in_specs=[SMEM, VMEM],
        out_specs=VMEM,
        scratch_shapes=[pltpu.SMEM(counts.shape, jnp.int32)],
        compiler_params=grant(8),
        cost_estimate=cost(1 << 20, 1 << 20),
        name="pack_hub",
    )(counts, data)


def pack_plain(data, counts, slots, bs, after):
    return pl.pallas_call(
        lambda *refs: pack_plain_kernel(slots, bs, *refs),
        out_shape=jax.ShapeDtypeStruct((counts.shape[0] - HUB_DEV, bs, data.shape[0]), BF),
        in_specs=[SMEM, VMEM, ANY],
        out_specs=VMEM,
        scratch_shapes=[pltpu.SMEM(counts.shape, jnp.int32)],
        compiler_params=grant(8),
        cost_estimate=cost(1 << 20, 1 << 20),
        name="pack_plain",
    )(counts, data, after)


class Gather:
    def __init__(self, near, hubs, table, sem, bs):
        below, own, above, crossing, turn = near
        size = own.shape[0] * bs
        z = lax.axis_index("var") % SIDE

        def copy(ref, at):
            rows = ref.shape[0] * bs
            return pltpu.make_async_copy(
                ref.reshape(rows, ref.shape[2]), table.at[pl.ds(at, rows), :], sem
            )

        self.choices = []
        for edge, usual, at in ((z == 0, below, 0), (z == SIDE - 1, above, 2 * size)):
            pair = [copy(crossing, at), copy(turn, at + crossing.shape[0] * bs)]
            self.choices.append((edge, copy(usual, at), pair))
        self.copies = [copy(own, size)]
        at = 3 * size
        for ref in hubs:
            for i in range(ref.shape[0]):
                self.copies.append(
                    pltpu.make_async_copy(
                        ref.at[i, pl.ds(0, HUB_DEV * bs), :],
                        table.at[pl.ds(at, HUB_DEV * bs), :],
                        sem,
                    )
                )
                at += HUB_DEV * bs

    def start(self):
        for copy in self.copies:
            copy.start()
        for edge, usual, pair in self.choices:
            for other in pair:
                pl.when(edge)(other.start)
            pl.when(jnp.logical_not(edge))(usual.start)

    def wait(self):
        for copy in self.copies:
            copy.wait()
        for _, usual, _ in self.choices:
            usual.wait()


def fill_lookup(pattern, ids, order, inverse, lookup):
    rows, slots = pattern.shape
    plain = rows - HUB_DEV
    base = lax.axis_index("var") * rows

    def clear(i, _):
        inverse[base + i] = -1
        return 0

    lax.fori_loop(0, 3 * rows, clear, 0)

    def mark(q, _):
        inverse[ids[q] + rows] = 3 * plain + q
        return 0

    lax.fori_loop(0, ids.shape[0], mark, 0)
    for side in range(3):

        def place(i, found):
            at = base + side * rows + i
            seen = inverse[at]
            inverse[at] = jnp.where(seen < 0, side * plain + found, seen)
            return found + jnp.where(seen < 0, 1, 0)

        lax.fori_loop(0, rows, place, jnp.int32(0))
    total = 3 * plain + ids.shape[0]
    for p in range(rows):
        for k in range(slots if p < HUB_DEV else HALF):
            c = inverse[pattern[order[p], k] + rows]
            lookup[slot_base(p, slots) + k] = jnp.clip(c, 0, total - 1)


def halves(tile_of, live):
    high, low = [], []
    for k in range(GROUP):
        tile = tile_of(k)
        if live is not None:
            tile = jnp.where(k < live, tile, 0.0)
        top = tile.astype(BF)
        high.append(top)
        low.append((tile - top.astype(F32)).astype(BF))
    return jnp.concatenate([jnp.concatenate(high, axis=1), jnp.concatenate(low, axis=1)], axis=0)


def image_group(left, lookup, table, start, bs):
    blocks = [table[aligned(lookup[start + k], bs), :] for k in range(GROUP)]
    both = jnp.dot(left, jnp.concatenate(blocks, axis=0), preferred_element_type=F32)
    return both[:bs] + both[bs:]


def hub_images(left_of, lookup, table, out, slots, bs):
    for p in range(HUB_DEV):
        total = None
        for start in range(p * slots, (p + 1) * slots, GROUP):
            part = image_group(left_of(start // GROUP), lookup, table, start, bs)
            total = part if total is None else total + part
        out[p * bs : (p + 1) * bs, :] = total.astype(BF)


def plain_images(left_of, lookup, table, out, slots, bs):
    first = HUB_DEV * slots

    def one(p, _):
        left = left_of(p)
        out[p] = image_group(left, lookup, table, first + p * HALF, bs).astype(BF)
        return 0

    lax.fori_loop(0, out.shape[0], one, 0, unroll=2)


def prep_kernel(counts, omega, left_hub, left, rows_out, order, tiles, part_sem, sems):
    rows, slots, _, _ = omega.shape
    share = rows_out.shape[1]
    row_order(counts, order, slots)
    part = aligned(lax.axis_index("samp"), share)
    whole, parts = [], []
    for p in range(rows):
        n = slots if p < HUB_DEV else HALF
        at = pl.ds(slot_base(p, slots), n)
        whole.append(
            pltpu.make_async_copy(omega.at[order[p], pl.ds(0, n)], tiles.at[at], sems.at[p])
        )
        parts.append(
            pltpu.make_async_copy(omega.at[order[p], pl.ds(0, n), part], rows_out.at[at], part_sem)
        )
    for move in whole + parts:
        move.start()
    for p in range(rows):
        whole[p].wait()
        start = slot_base(p, slots)
        live = None if p < HUB_DEV else counts[order[p]]
        for s in range(start, start + (slots if p < HUB_DEV else HALF), GROUP):
            g = s // GROUP
            if p < HUB_DEV:
                left_hub[g] = halves(lambda k: tiles[s + k], live)
            else:
                left[g - left_hub.shape[0]] = halves(lambda k: tiles[s + k], live)
    for move in parts:
        move.wait()


def prep(counts, omega, part_count):
    rows, slots, bs, _ = omega.shape
    total = HUB_DEV * slots + (rows - HUB_DEV) * HALF
    return pl.pallas_call(
        prep_kernel,
        out_shape=(
            jax.ShapeDtypeStruct((HUB_DEV * slots // GROUP, 2 * bs, GROUP * bs), BF),
            jax.ShapeDtypeStruct((rows - HUB_DEV, 2 * bs, GROUP * bs), BF),
            jax.ShapeDtypeStruct((total, bs // part_count, bs), F32),
        ),
        in_specs=[SMEM, ANY],
        out_specs=(VMEM, VMEM, VMEM),
        scratch_shapes=[
            pltpu.SMEM((rows,), jnp.int32),
            pltpu.VMEM((total, bs, bs), F32),
            pltpu.SemaphoreType.DMA,
            pltpu.SemaphoreType.DMA((rows,)),
        ],
        compiler_params=grant(48),
        cost_estimate=cost(1 << 24, 12 << 20),
        name="prep",
    )(counts, omega)


def first_hub_kernel(*refs):
    counts, pattern, ids, left = refs[:4]
    near, hubs = refs[4:9], refs[9:14]
    out, lookup, table = refs[14:17]
    order, inverse, sem = refs[17:]
    slots = pattern.shape[1]
    bs = left.shape[1] // 2
    row_order(counts, order, slots)
    gather = Gather(near, hubs, table, sem, bs)
    gather.start()
    fill_lookup(pattern, ids, order, inverse, lookup)
    gather.wait()
    hub_images(lambda g: left[g], lookup, table, out, slots, bs)


def first_hub(counts, pattern, ids, left, near, hubs):
    rows, slots = pattern.shape
    total = HUB_DEV * slots + (rows - HUB_DEV) * HALF
    bs = left.shape[1] // 2
    local = hubs[0].shape[2]
    table = (3 * (rows - HUB_DEV) + SIDE * SIDE * HUB_DEV) * bs
    return pl.pallas_call(
        first_hub_kernel,
        out_shape=(
            jax.ShapeDtypeStruct((HUB_DEV * bs, local), BF),
            jax.ShapeDtypeStruct((total,), jnp.int32),
            jax.ShapeDtypeStruct((table, local), BF),
        ),
        in_specs=[SMEM, SMEM, SMEM, VMEM] + [ANY] * 10,
        out_specs=(VMEM, SMEM, VMEM),
        scratch_shapes=[
            pltpu.SMEM((rows,), jnp.int32),
            pltpu.SMEM((rows * (SIDE * SIDE + 2),), jnp.int32),
            pltpu.SemaphoreType.DMA,
        ],
        compiler_params=grant(12),
        cost_estimate=cost(1 << 28, 12 << 20),
        name="hub_first",
    )(counts, pattern, ids, left, *near, *hubs)


def first_plain_kernel(slots, lookup, left, table, _, out):
    bs = out.shape[1]
    plain_images(lambda p: left[p], lookup, table, out, slots, bs)


def first_plain(lookup, left, table, slots, after):
    bs = left.shape[1] // 2
    plain = (lookup.shape[0] - HUB_DEV * slots) // HALF
    return pl.pallas_call(
        lambda *refs: first_plain_kernel(slots, *refs),
        out_shape=jax.ShapeDtypeStruct((plain, bs, table.shape[1]), BF),
        in_specs=[SMEM, VMEM, VMEM, ANY],
        out_specs=VMEM,
        compiler_params=grant(12),
        cost_estimate=cost(1 << 29, 10 << 20),
        name="plain_first",
    )(lookup, left, table, after)


def wire_scales(tail, scales):
    exponent = tail.astype(jnp.int32).astype(F32).reshape(scales.shape)
    scales[...] = jnp.exp2(exponent) * (1.0 / LEVELS)


def to_wire(read, out, scales, total):
    scales[...] = jnp.ones_like(scales)

    def peak(s, _):
        scales[pl.ds(s, 1), :] = jnp.max(jnp.abs(read(s)), axis=0, keepdims=True)
        return 0

    lax.fori_loop(0, total, peak, 0, unroll=8)
    exponent = jnp.ceil(jnp.log2(jnp.maximum(scales[...], TINY)))
    tail = exponent.reshape(-1, *out.shape[1:])
    out[total:] = tail.astype(jnp.int32).astype(WIRE)
    scales[...] = jnp.exp2(-exponent) * LEVELS

    def put(s, _):
        out[s] = jnp.round(read(s) * scales[pl.ds(s, 1), :]).astype(jnp.int32).astype(WIRE)
        return 0

    lax.fori_loop(0, total, put, 0, unroll=8)


def wire_shape(total, share, bs):
    return (total + -(-total // share), share, bs)


def later_kernel(slots, hub, *refs):
    counts, lookup, mine, partner, table, _, out = refs[:7]
    order, levels, tails, scales, sem = refs[7:]
    total, bs = lookup.shape[0], levels.shape[1]
    share = mine.shape[2]
    first = 0 if hub else HUB_DEV * slots
    row_order(counts, order, slots)
    part = lax.axis_index("samp")
    moves = []
    for j in range(SIDE):
        for ref, core in ((mine, part % CORES), (partner, (part + 1) % CORES)):
            at = ((part // CORES + j) % SIDE) * CORES + core
            moves.append(
                pltpu.make_async_copy(
                    ref.at[j, pl.ds(first, levels.shape[0])],
                    levels.at[:, aligned(at, share), :],
                    sem,
                )
            )
            moves.append(
                pltpu.make_async_copy(
                    ref.at[j, pl.ds(total, mine.shape[1] - total)], tails.at[at], sem
                )
            )
    for move in moves:
        move.start()
    for move in moves:
        move.wait()
    for g in range(SIDE * CORES):
        wire_scales(tails[g], scales.at[g])

    def tile_of(s):
        rows = [
            levels[s, g * share : (g + 1) * share, :].astype(jnp.int32).astype(F32)
            * scales[g, pl.ds(first + s, 1), :]
            for g in range(SIDE * CORES)
        ]
        return jnp.concatenate(rows, axis=0)

    if hub:
        hub_images(
            lambda g: halves(lambda k: tile_of(g * GROUP + k), None), lookup, table, out, slots, bs
        )
    else:
        plain_images(
            lambda p: halves(lambda k: tile_of(p * HALF + k), counts[order[HUB_DEV + p]]),
            lookup,
            table,
            out,
            slots,
            bs,
        )


def later_image(counts, lookup, mine, partner, table, slots, after):
    total = lookup.shape[0]
    plain = counts.shape[0] - HUB_DEV
    _, long, share, bs = mine.shape
    local = table.shape[1]
    groups = SIDE * CORES
    hub = after is None
    count = HUB_DEV * slots if hub else plain * HALF
    return pl.pallas_call(
        lambda *refs: later_kernel(slots, hub, *refs),
        out_shape=jax.ShapeDtypeStruct(
            (HUB_DEV * bs, local) if hub else (plain, bs, local), BF
        ),
        in_specs=[SMEM, SMEM, ANY, ANY, VMEM, ANY],
        out_specs=VMEM,
        scratch_shapes=[
            pltpu.SMEM(counts.shape, jnp.int32),
            pltpu.VMEM((count, bs, bs), WIRE),
            pltpu.VMEM((groups, long - total, share, bs), WIRE),
            pltpu.VMEM((groups, (long - total) * share, bs), F32),
            pltpu.SemaphoreType.DMA,
        ],
        compiler_params=grant(16),
        cost_estimate=cost(1 << 28 if hub else 1 << 29, (2 if hub else 8) << 20),
        name="hub_later" if hub else "plain_later",
    )(counts, lookup, mine, partner, table, counts if hub else after)


def groups(slots, plain, term):
    for p in range(HUB_DEV):
        for start in range(p * slots, (p + 1) * slots, GROUP):
            term(start, 3 * plain + p)

    def step(p, _):
        term(HUB_DEV * slots + p * HALF, plain + p)
        return 0

    lax.fori_loop(0, plain, step, 0, unroll=2)


def product(own, lookup, table, start, bs):
    right = [table[aligned(lookup[start + k], bs), :] for k in range(GROUP)]
    return lax.dot_general(
        own, jnp.concatenate(right, axis=0), (((1,), (1,)), ((), ())), preferred_element_type=F32
    )


def firsts_kernel(slots, lookup, x_table, m_own, m_hub, out):
    plain, bs, _ = m_own.shape
    for p in range(HUB_DEV):
        for start in range(p * slots, (p + 1) * slots, GROUP):
            own = m_hub[p * bs : (p + 1) * bs, :]
            out[start // GROUP] = product(own, lookup, x_table, start, bs)

    def step(p, _):
        start = HUB_DEV * slots + p * HALF
        out[HUB_DEV * slots // GROUP + p] = product(m_own[p], lookup, x_table, start, bs)
        return 0

    lax.fori_loop(0, plain, step, 0, unroll=2)


def first_terms(lookup, table, m_own, m_hub, slots):
    bs = m_own.shape[1]
    return pl.pallas_call(
        lambda *refs: firsts_kernel(slots, *refs),
        out_shape=jax.ShapeDtypeStruct((lookup.shape[0] // GROUP, bs, GROUP * bs), F32),
        in_specs=[SMEM, VMEM, VMEM, VMEM],
        out_specs=VMEM,
        compiler_params=grant(12),
        cost_estimate=cost(1 << 29, 10 << 20),
        name="firsts",
    )(lookup, table, m_own, m_hub)


def gradient_kernel(scale, slots, *refs):
    lookup, x_table, firsts = refs[:3]
    near, hubs = refs[3:8], refs[8:13]
    keep, send, m_table, sem = refs[13:]
    plain, bs, _ = near[1].shape
    gather = Gather(near, hubs, m_table, sem, bs)
    gather.start()
    gather.wait()
    part = lax.axis_index("samp")
    y, core = part // CORES, part % CORES
    share = keep.shape[2]

    def group(start, own):
        term = product(x_table[aligned(own, bs), :], lookup, m_table, start, bs)
        both = (firsts[start // GROUP] + term) * scale
        for k in range(GROUP):
            tile = both[:, k * bs : (k + 1) * bs].reshape(SIDE, CORES, share, bs)
            even, odd = tile[:, 0], tile[:, 1]
            stay = jnp.where(core == 0, even, odd)
            leave = jnp.where(core == 0, odd, even)
            for g in range(SIDE):
                to = (g + SIDE - y) % SIDE
                keep[to, start + k] = stay[g]
                send[to, start + k] = leave[g]

    groups(slots, plain, group)


def gradient(lookup, table, firsts, near, hubs, scale, slots, part_count):
    total = lookup.shape[0]
    bs = firsts.shape[1]
    shape = jax.ShapeDtypeStruct((SIDE, total, bs // part_count, bs), F32)
    return pl.pallas_call(
        lambda *refs: gradient_kernel(scale, slots, *refs),
        out_shape=(shape, shape),
        in_specs=[SMEM, VMEM, VMEM] + [ANY] * 10,
        out_specs=(VMEM, VMEM),
        scratch_shapes=[pltpu.VMEM(table.shape, BF), pltpu.SemaphoreType.DMA],
        compiler_params=grant(20),
        cost_estimate=cost(1 << 30, 16 << 20),
        name="gradient",
    )(lookup, table, firsts, *near, *hubs)


def add_kernel(keep, other, own, *refs):
    sends, total_sum, scales = refs[:-2], refs[-2], refs[-1]
    total = own.shape[0]
    own[...] = keep[0] + other[0]
    for j, ref in enumerate(sends):
        total_sum[...] = keep[j + 1] + other[j + 1]
        to_wire(lambda s: total_sum[s], ref, scales, total)


def add_cores(keep, other):
    side, total, share, bs = keep.shape
    wire = jax.ShapeDtypeStruct(wire_shape(total, share, bs), WIRE)
    return pl.pallas_call(
        add_kernel,
        out_shape=(jax.ShapeDtypeStruct((total, share, bs), F32),) + (wire,) * (side - 1),
        in_specs=[VMEM, VMEM],
        out_specs=(VMEM,) * side,
        scratch_shapes=[
            pltpu.VMEM((total, share, bs), F32),
            pltpu.VMEM(((wire.shape[0] - total) * share, bs), F32),
        ],
        compiler_params=grant(16),
        name="add_cores",
    )(keep, other)


def new_tile(tile, slope, leading, live, part, share):
    stepped = tile - STEP_SIZE * slope
    edge = STEP_SIZE * PENALTY
    shrunk = stepped - jnp.minimum(jnp.maximum(stepped, -edge), edge)
    if leading:
        shape = stepped.shape
        row = part * share + lax.broadcasted_iota(jnp.int32, shape, 0)
        col = lax.broadcasted_iota(jnp.int32, shape, 1)
        barrier = 0.5 * (stepped + jnp.sqrt(stepped * stepped + 4.0 * STEP_SIZE))
        shrunk = jnp.where(row == col, barrier, shrunk)
    return jnp.where(live, shrunk, 0.0)


def prox_kernel(last, slots, counts, tiles, own, *refs):
    sends = refs[: SIDE - 1]
    outs = refs[SIDE - 1 : -2]
    order, scales = refs[-2:]
    rows = order.shape[0]
    row_order(counts, order, slots)
    part = lax.axis_index("samp")
    total, share, bs = own.shape
    for j, ref in enumerate(sends):
        wire_scales(ref[total:], scales.at[j])

    def slot(row, s, k, n):
        slope = own[s]
        for j, ref in enumerate(sends):
            slope = slope + ref[s].astype(jnp.int32).astype(F32) * scales[j, pl.ds(s, 1), :]
        value = new_tile(tiles[s], slope, k == 0, k < n, part, share)
        if last:
            outs[0][row, k] = value
        else:
            outs[0][s] = value

    for p in range(HUB_DEV):
        for k in range(slots):
            slot(order[p], p * slots + k, k, slots)

    def plain(p, _):
        row = order[HUB_DEV + p]
        n = counts[row]
        for k in range(HALF):
            slot(row, HUB_DEV * slots + p * HALF + k, k, n)
        if last:
            for k in range(HALF, slots):
                outs[0][row, k] = jnp.zeros((share, bs), F32)
        return 0

    lax.fori_loop(0, rows - HUB_DEV, plain, 0, unroll=2)
    if not last:
        to_wire(lambda s: outs[0][s], outs[1], scales.at[0], total)


def prox(counts, tiles, terms, slots, last):
    rows = counts.shape[0]
    total, share, bs = tiles.shape
    wire = wire_shape(total, share, bs)
    if last:
        outs = (jax.ShapeDtypeStruct((rows, slots, share, bs), F32),)
    else:
        outs = (jax.ShapeDtypeStruct((total, share, bs), F32), jax.ShapeDtypeStruct(wire, WIRE))
    return pl.pallas_call(
        lambda *refs: prox_kernel(last, slots, *refs),
        out_shape=outs,
        in_specs=[SMEM] + [VMEM] * 5,
        out_specs=(VMEM,) * len(outs),
        scratch_shapes=[
            pltpu.SMEM((rows,), jnp.int32),
            pltpu.VMEM((SIDE - 1, (wire[0] - total) * share, bs), F32),
        ],
        compiler_params=grant(16),
        name="prox_last" if last else "prox",
    )(counts, tiles, *terms)


def share_near(value):
    last = lax.axis_size("var") // SIDE - 1
    size = lax.axis_size("var")
    far = SIDE - 1
    direct, there, over = [], [], []
    for x in range(last):
        low, high = x * SIDE, (x + 1) * SIDE
        direct += [(low + far, high), (high, low + far)]
        there += [(low + far, low), (high, high + far)]
        over += [(low, high), (high + far, low + far)]
    half = value.shape[0] * 5 // 14
    crossing = lax.ppermute(value[:half], "var", direct)
    turn = lax.ppermute(value[half:], "var", there)
    turn = lax.ppermute(turn, "var", over)
    up = [(i, i + 1) for i in range(size - 1) if (i + 1) % SIDE]
    below = lax.ppermute(value, "var", up)
    above = lax.ppermute(value, "var", [(j, i) for i, j in up])
    return below, value, above, crossing, turn


def share_hubs(value):
    by_z = [value] + [lax.ppermute(value, "var", var_shift(0, d)) for d in (1, -1, 2)]
    column = jnp.stack(by_z)
    half = SIDE // 2
    ahead = lax.ppermute(column, "var", var_shift(1, 0))
    behind = lax.ppermute(column, "var", var_shift(-1, 0))
    across = [
        lax.ppermute(ahead[:half], "var", var_shift(1, 0)),
        lax.ppermute(behind[half:], "var", var_shift(-1, 0)),
    ]
    return [column, ahead, behind] + across


def along_y(near, across, other, step):
    across = lax.ppermute(across, "samp", samp_shift(2, 0))
    near = lax.ppermute(near, "samp", samp_shift(step, 0))
    other = lax.ppermute(other, "samp", samp_shift(-step, 0))
    return [near, across, other]


def per_device(data, omega, pattern, counts):
    parts = lax.axis_size("samp")
    _, slots, bs, _ = omega.shape
    scale = 0.5 / (data.shape[0] * parts)
    x_hub = pack_hub(data, counts, slots, bs)
    x_hubs = share_hubs(x_hub)
    x_own = pack_plain(data, counts, slots, bs, x_hub)
    x_near = share_near(x_own)
    left_hub, left, tiles = prep(counts, omega, parts)
    ids = jnp.concatenate([g[:, HUB_DEV * bs : HUB_DEV * bs + HUB_DEV, 0] for g in x_hubs])
    ids = ids.reshape(-1).astype(jnp.int32)
    for iteration in range(ITERS):
        if iteration == 0:
            m_hub, lookup, table = first_hub(counts, pattern, ids, left_hub, x_near, x_hubs)
        else:
            mine = jnp.stack([sent] + along_y(sent, sent, sent, -1))
            partner = lax.ppermute(mine, "samp", samp_shift(0, 1))
            m_hub = later_image(counts, lookup, mine, partner, table, slots, None)
        m_hubs = share_hubs(m_hub)
        if iteration == 0:
            m_own = first_plain(lookup, left, table, slots, m_hub)
        else:
            m_own = later_image(counts, lookup, mine, partner, table, slots, m_hub)
        m_near = share_near(m_own)
        firsts = first_terms(lookup, table, m_own, m_hub, slots)
        keep, leave = gradient(lookup, table, firsts, m_near, m_hubs, scale, slots, parts)
        other = lax.ppermute(leave, "samp", samp_shift(0, 1))
        own, up, across, down = add_cores(keep, other)
        terms = [own] + along_y(up, across, down, 1)
        if iteration < ITERS - 1:
            tiles, sent = prox(counts, tiles, terms, slots, False)
        else:
            (tiles,) = prox(counts, tiles, terms, slots, True)
    return tiles


def solution(mesh):
    placed = (P("samp", "var"), P("var", None, None, None), P("var", None), P("var"))
    return jax.shard_map(
        per_device,
        mesh=mesh,
        in_specs=placed,
        out_specs=P("var", None, "samp", None),
        check_vma=False,
    )
```
